32 devices in a mesh: bias: 2 (over x), ea: 16 (over z, y, core).
Axes of the slice: x: 2, y: 2, z: 4, core: 2. Of those that a mesh axis runs over, the one named last changes fastest.
Arguments:
- g_lesser: bfloat16 [512, 2, 256, 256], P(('bias', 'ea')), parts along dimension 0, may hold values from -6 to 6
- g_greater: bfloat16 [512, 2, 256, 256], P(('bias', 'ea')), parts along dimension 0, may hold values from -6 to 6
- g_free: bfloat16 [512, 2, 256, 256], P(('bias', 'ea')), parts along dimension 0, may hold values from -3 to 3
- coulomb: bfloat16 [256, 256], replicated, may hold values from -0.375 to 0.375
Outputs:
- g_new: bfloat16 [512, 2, 256, 256], P(('bias', 'ea')), parts along dimension 0
The draws below stay inside these ranges and needn't reach their ends.
There are 2 independent parts, one for each index of `bias`. The reference program is written for one: setup_inputs(seed, part) draws one part's arguments, and reference() takes and returns one part's arrays. A program takes and returns all parts, laid end to end along the dimension named above; an argument that names none is the same for every part. Nothing has to cross between parts.
All inputs are finite; a program needn't handle non-finite values.
Results may differ from the reference program's by a relative error of at most 0.022.
Values may be sent and summed in bfloat16 or wider, within the bound.
No kernel may reach another device: no remote copies, remote signals or barrier semaphores. Data moves between devices by JAX's collectives and lax.ppermute only.
A program may use at most 192 MiB of HBM per device.

```python
import jax
import jax.numpy as jnp

NO = 256
NE = 256


def levels(rng, extent, shards, least, top_value):
    def one(position, parts):
        steps = jax.random.uniform(jax.random.fold_in(jax.random.fold_in(rng, 6), position), (parts,), jnp.float32, least / len(shards), top_value / len(shards))
        return jnp.repeat(jnp.exp(steps), extent[position] // parts).reshape((-1,) + (1,) * (len(extent) - position - 1))

    gain = one(*shards[0])
    for cut in shards[1:]:
        gain = gain * one(*cut)
    return gain


def gaussian(own_key, shape, width, reach, split=(), held_as=jnp.bfloat16):
    level = levels(own_key, shape, split, -0.22, 0.18) if split else 1.0
    entries = jax.random.normal(own_key, shape, jnp.float32) * width * level
    return jnp.minimum(jnp.maximum(entries, -reach), reach).astype(held_as)


def setup_inputs(seed: int = 0, part: int = 0) -> dict:
    key_list = jax.random.split(jax.random.key(seed), 5)
    part_keys = jax.random.split(jax.random.fold_in(key_list[4], part), 5)
    g_lesser = gaussian(part_keys[0], (NE, 2, NO, NO), 1.0, 6.0, ((0, 16),))
    g_greater = gaussian(part_keys[1], (NE, 2, NO, NO), 1.0, 6.0, ((0, 16),))
    g_free = gaussian(part_keys[2], (NE, 2, NO, NO), 0.5, 3.0, ((0, 16),))
    coulomb = gaussian(key_list[3], (NO, NO), NO ** -0.5, 0.375)
    return dict(g_lesser=g_lesser, g_greater=g_greater, g_free=g_free, coulomb=coulomb)


def as_complex(block):
    return block[:, 0].astype(jnp.float32) + 1j * block[:, 1].astype(jnp.float32)


def batched(left, right):
    return jnp.einsum("eij,ejk->eik", left.astype(jnp.float32), right.astype(jnp.float32))


def reference(g_lesser, g_greater, g_free, coulomb):
    length = 2 * NE
    lesser = as_complex(g_lesser)
    greater_t = jnp.swapaxes(as_complex(g_greater), 1, 2)
    spec_lesser = jnp.fft.fft(lesser, n=length, axis=0)
    spec_greater = jnp.fft.ifft(greater_t, n=length, axis=0) * length
    polar = jnp.fft.ifft(spec_lesser * spec_greater, axis=0)[:NE] / NE
    polar_real = polar.real.astype(jnp.bfloat16)
    polar_imag = polar.imag.astype(jnp.bfloat16)
    volts = coulomb.astype(jnp.float32)
    mixed_real = jnp.einsum("eij,jk->eik", polar_real.astype(jnp.float32), volts).astype(jnp.bfloat16)
    mixed_imag = jnp.einsum("eij,jk->eik", polar_imag.astype(jnp.float32), volts).astype(jnp.bfloat16)
    square_real = batched(mixed_real, mixed_real) - batched(mixed_imag, mixed_imag)
    square_imag = batched(mixed_real, mixed_imag) + batched(mixed_imag, mixed_real)
    inner_real = (mixed_real.astype(jnp.float32) + square_real).astype(jnp.bfloat16)
    inner_imag = (mixed_imag.astype(jnp.float32) + square_imag).astype(jnp.bfloat16)
    screen_real = (volts[None] + jnp.einsum("ij,ejk->eik", volts, inner_real.astype(jnp.float32))).astype(jnp.bfloat16)
    screen_imag = jnp.einsum("ij,ejk->eik", volts, inner_imag.astype(jnp.float32)).astype(jnp.bfloat16)
    screen = screen_real.astype(jnp.float32) + 1j * screen_imag.astype(jnp.float32)
    spec_screen = jnp.fft.fft(screen, n=length, axis=0)
    sigma = jnp.fft.ifft(spec_lesser * spec_screen, axis=0)[:NE] / NE
    sigma_real = sigma.real.astype(jnp.bfloat16)
    sigma_imag = sigma.imag.astype(jnp.bfloat16)
    free_real = g_free[:, 0]
    free_imag = g_free[:, 1]
    right_real = (batched(sigma_real, free_real) - batched(sigma_imag, free_imag)).astype(jnp.bfloat16)
    right_imag = (batched(sigma_real, free_imag) + batched(sigma_imag, free_real)).astype(jnp.bfloat16)
    out_real = free_real.astype(jnp.float32) + batched(free_real, right_real) - batched(free_imag, right_imag)
    out_imag = free_imag.astype(jnp.float32) + batched(free_real, right_imag) + batched(free_imag, right_real)
    return jnp.stack([out_real, out_imag], axis=1).astype(jnp.bfloat16)
```

```python
import functools
import math

import jax
import jax.numpy as jnp
from jax import lax
from jax.experimental import pallas as pl
from jax.experimental.pallas import tpu as pltpu
from jax.sharding import PartitionSpec as P

BF = jnp.bfloat16
F32 = jnp.float32


def dot(left, right):
    return jnp.dot(left, right, preferred_element_type=F32)


def swap_matrix(block):
    size = block * block
    row = lax.broadcasted_iota(jnp.int32, (size, size), 0)
    col = lax.broadcasted_iota(jnp.int32, (size, size), 1)
    return ((row % block) * block + row // block == col).astype(BF)


def spectral_tables(count):
    length = 2 * count
    freq = jnp.arange(length, dtype=jnp.int32)
    places = jnp.arange(count, dtype=jnp.int32)
    angle = (freq[:, None] * places[None, :] % length).astype(F32) * (2.0 * math.pi / length)
    cosine, sine = jnp.cos(angle), jnp.sin(angle)

    def joined(sign):
        top = jnp.concatenate([cosine, -sign * sine], axis=1)
        return jnp.concatenate([top, jnp.concatenate([sign * sine, cosine], axis=1)], axis=0)

    forward = joined(-1.0)
    return (
        forward.astype(BF),
        joined(1.0).astype(BF),
        (forward.T * (1.0 / (length * count))).astype(BF),
    )


def pack_rows_kernel(swap_ref, in_ref, out_ref):
    block = in_ref.shape[0]
    size = in_ref.shape[-1]
    for j in range(out_ref.shape[0]):
        piece = in_ref[:, 0, block * j : block * (j + 1), :].reshape(block * block, size)
        out_ref[j, 0] = dot(swap_ref[...], piece).astype(BF).reshape(block, block, size)


def pack_rows(swap, g):
    block, _, size, _ = g.shape
    groups = size // block
    per = 4
    return pl.pallas_call(
        pack_rows_kernel,
        grid=(2, groups // per),
        in_specs=[
            pl.BlockSpec(swap.shape, lambda r, j: (0, 0)),
            pl.BlockSpec((block, 1, block * per, size), lambda r, j: (0, r, j, 0)),
        ],
        out_specs=pl.BlockSpec((per, 1, block, block, size), lambda r, j: (j, r, 0, 0, 0)),
        out_shape=jax.ShapeDtypeStruct((groups, 2, block, block, size), BF),
        cost_estimate=pl.CostEstimate(
            flops=4 * block * size**3, bytes_accessed=4 * g.size, transcendentals=0
        ),
        name="pack_rows",
    )(swap, g)


def pack_columns_kernel(swap_ref, eye_ref, in_ref, out_ref, turned):
    block = in_ref.shape[0]
    size = in_ref.shape[2]
    for e in range(block):
        turned[e] = lax.dot_general(
            eye_ref[...], in_ref[e, 0], (((1,), (1,)), ((), ())), preferred_element_type=F32
        ).astype(BF)
    for j in range(out_ref.shape[0]):
        piece = turned[:, block * j : block * (j + 1), :].reshape(block * block, size)
        out_ref[j, 0] = dot(swap_ref[...], piece).astype(BF).reshape(block, block, size)


def pack_columns(swap, g):
    block, _, size, _ = g.shape
    groups = size // block
    lanes = 128
    per = lanes // block
    eye = jnp.eye(lanes, dtype=BF)
    return pl.pallas_call(
        pack_columns_kernel,
        grid=(2, size // lanes),
        in_specs=[
            pl.BlockSpec(swap.shape, lambda r, j: (0, 0)),
            pl.BlockSpec(eye.shape, lambda r, j: (0, 0)),
            pl.BlockSpec((block, 1, size, lanes), lambda r, j: (0, r, 0, j)),
        ],
        out_specs=pl.BlockSpec((per, 1, block, block, size), lambda r, j: (j, r, 0, 0, 0)),
        out_shape=jax.ShapeDtypeStruct((groups, 2, block, block, size), BF),
        scratch_shapes=[pltpu.VMEM((block, lanes, size), BF)],
        cost_estimate=pl.CostEstimate(
            flops=8 * block * size**3, bytes_accessed=4 * g.size, transcendentals=0
        ),
        name="pack_columns",
    )(swap, eye, g)


def stacked(ref):
    size = ref.shape[-1]
    return jnp.concatenate(
        [ref[:, 0, 0].reshape(-1, size), ref[:, 1, 0].reshape(-1, size)], axis=0
    )


def unstack(out_ref, value):
    count = value.shape[0] // 2
    shape = (out_ref.shape[0],) + out_ref.shape[3:]
    value = value.astype(BF)
    out_ref[:, 0, 0] = value[:count].reshape(shape)
    out_ref[:, 1, 0] = value[count:].reshape(shape)


def product(left, right):
    half = left.shape[0] // 2
    lr, li = left[:half], left[half:]
    rr, ri = right[:half], right[half:]
    return jnp.concatenate([lr * rr - li * ri, lr * ri + li * rr], axis=0).astype(BF)


def polar_kernel(minus_ref, plus_ref, back_ref, lesser_ref, greater_ref, out_ref, spec_ref):
    spec_lesser = dot(minus_ref[...], stacked(lesser_ref))
    spec_ref[0] = spec_lesser.astype(BF)
    spec_greater = dot(plus_ref[...], stacked(greater_ref))
    unstack(out_ref, dot(back_ref[...], product(spec_lesser, spec_greater)))


def fold_kernel(minus_ref, back_ref, spec_ref, screen_ref, out_ref):
    spec_screen = dot(minus_ref[...], stacked(screen_ref))
    unstack(out_ref, dot(back_ref[...], product(spec_ref[0].astype(F32), spec_screen)))


def whole_spec(array):
    return pl.BlockSpec(array.shape, lambda *_: (0,) * array.ndim)


def row_spec(array):
    shape = array.shape
    return pl.BlockSpec((shape[0], 2, 1) + shape[3:], lambda a: (0, 0, a, 0, 0))


def polarization(tables, lesser, greater):
    minus, plus, back = tables
    rows, size = lesser.shape[2], lesser.shape[4]
    spec_shape = (rows, minus.shape[0], size)
    return pl.pallas_call(
        polar_kernel,
        grid=(rows,),
        in_specs=[whole_spec(minus), whole_spec(plus), whole_spec(back), row_spec(lesser), row_spec(greater)],
        out_specs=[row_spec(lesser), pl.BlockSpec((1,) + spec_shape[1:], lambda a: (a, 0, 0))],
        out_shape=[
            jax.ShapeDtypeStruct(lesser.shape, BF),
            jax.ShapeDtypeStruct(spec_shape, BF),
        ],
        cost_estimate=pl.CostEstimate(
            flops=6 * rows * minus.size * size,
            bytes_accessed=6 * lesser.size + 2 * rows * minus.shape[0] * size,
            transcendentals=0,
        ),
        name="polarization",
    )(minus, plus, back, lesser, greater)


def self_energy(tables, spec, screen):
    minus, _, back = tables
    rows, size = screen.shape[2], screen.shape[4]
    return pl.pallas_call(
        fold_kernel,
        grid=(rows,),
        in_specs=[
            whole_spec(minus),
            whole_spec(back),
            pl.BlockSpec((1,) + spec.shape[1:], lambda a: (a, 0, 0)),
            row_spec(screen),
        ],
        out_specs=row_spec(screen),
        out_shape=jax.ShapeDtypeStruct(screen.shape, BF),
        cost_estimate=pl.CostEstimate(
            flops=4 * rows * minus.size * size,
            bytes_accessed=4 * screen.size + 2 * spec.size,
            transcendentals=0,
        ),
        name="self_energy",
    )(minus, back, spec, screen)


def gather_matrices(swap_ref, in_ref, whole):
    block, size = in_ref.shape[2], in_ref.shape[4]

    @pl.loop(0, in_ref.shape[0])
    def _(s):
        for r in range(2):
            piece = in_ref[s, r].reshape(block * block, size)
            whole[r, :, s] = dot(swap_ref[...], piece).astype(BF).reshape(block, block, size)


def screen_kernel(swap_ref, coulomb_ref, in_ref, out_ref, whole):
    size = coulomb_ref.shape[0]
    block = in_ref.shape[2]
    gather_matrices(swap_ref, in_ref, whole)
    volts = coulomb_ref[...]

    @pl.loop(0, block)
    def _(w):
        mr = dot(whole[0, w].reshape(size, size), volts).astype(BF)
        mi = dot(whole[1, w].reshape(size, size), volts).astype(BF)
        nr = (mr.astype(F32) + (dot(mr, mr) - dot(mi, mi))).astype(BF)
        ni = (mi.astype(F32) + (dot(mr, mi) + dot(mi, mr))).astype(BF)
        wr = (volts.astype(F32) + dot(volts, nr)).astype(BF)
        wi = dot(volts, ni).astype(BF)
        whole[0, w] = wr.reshape(whole.shape[2:])
        whole[1, w] = wi.reshape(whole.shape[2:])

    @pl.loop(0, in_ref.shape[0])
    def _(d):
        for r in range(2):
            piece = whole[r, :, d].reshape(block * block, size)
            out_ref[d, r] = dot(swap_ref[...], piece).astype(BF).reshape(block, block, size)


def screened(swap, coulomb, polar):
    groups, _, block, _, size = polar.shape
    return pl.pallas_call(
        screen_kernel,
        out_shape=jax.ShapeDtypeStruct(polar.shape, BF),
        scratch_shapes=[pltpu.VMEM((2, block, groups, block, size), BF)],
        cost_estimate=pl.CostEstimate(
            flops=20 * block * size**3, bytes_accessed=4 * polar.size, transcendentals=0
        ),
        name="screened",
    )(swap, coulomb, polar)


def dyson_kernel(swap_ref, sigma_ref, free_ref, out_ref, whole):
    size = free_ref.shape[-1]
    e = pl.program_id(0)

    @pl.when(e == 0)
    def _():
        gather_matrices(swap_ref, sigma_ref, whole)

    sr = whole[0, e].reshape(size, size)
    si = whole[1, e].reshape(size, size)
    fr, fi = free_ref[0, 0], free_ref[0, 1]
    rr = (dot(sr, fr) - dot(si, fi)).astype(BF)
    ri = (dot(sr, fi) + dot(si, fr)).astype(BF)
    out_ref[0, 0] = (fr.astype(F32) + dot(fr, rr) - dot(fi, ri)).astype(BF)
    out_ref[0, 1] = (fi.astype(F32) + dot(fr, ri) + dot(fi, rr)).astype(BF)


def dyson(swap, sigma, free):
    groups, _, block, _, size = sigma.shape
    energy_spec = pl.BlockSpec((1, 2, size, size), lambda e: (e, 0, 0, 0))
    return pl.pallas_call(
        dyson_kernel,
        grid=(block,),
        in_specs=[whole_spec(swap), whole_spec(sigma), energy_spec],
        out_specs=energy_spec,
        out_shape=jax.ShapeDtypeStruct(free.shape, BF),
        scratch_shapes=[pltpu.VMEM((2, block, groups, block, size), BF)],
        cost_estimate=pl.CostEstimate(
            flops=18 * block * size**3, bytes_accessed=6 * free.size, transcendentals=0
        ),
        name="dyson",
    )(swap, sigma, free)


def dft_tables(length, count):
    freq = jnp.arange(length, dtype=jnp.int32)
    places = jnp.arange(count, dtype=jnp.int32)
    phase = freq[:, None] * places[None, :] % length
    angle = phase.astype(jnp.float32) * (2.0 * math.pi / length)
    cosine = jnp.cos(angle)
    sine = jnp.sin(angle)
    stacked = jnp.concatenate([cosine, sine], axis=0)
    upper = stacked.astype(jnp.bfloat16)
    lower = (stacked - upper.astype(jnp.float32)).astype(jnp.bfloat16)
    backward = jnp.concatenate([cosine.T, sine.T], axis=0)
    return (upper, lower, backward)


def forward(tables, block, sign):
    upper, lower = tables
    length = upper.shape[0] // 2
    real_part = block[:, 0].reshape(block.shape[0], -1)
    imag_part = block[:, 1].reshape(block.shape[0], -1)
    width = real_part.shape[1]
    joined = jnp.concatenate([real_part, imag_part], axis=1)
    result = jnp.dot(upper, joined, preferred_element_type=jnp.float32)
    result = result + jnp.dot(lower, joined, preferred_element_type=jnp.float32)
    cos_real = result[:length, :width]
    cos_imag = result[:length, width:]
    sin_real = result[length:, :width]
    sin_imag = result[length:, width:]
    return (cos_real - sign * sin_imag, cos_imag + sign * sin_real)


def inverse(backward, real_part, imag_part, scale):
    count = backward.shape[0] // 2
    width = real_part.shape[1]
    joined = jnp.concatenate([real_part, imag_part], axis=1)
    result = jnp.dot(
        backward, joined, precision=lax.Precision.HIGH, preferred_element_type=jnp.float32
    )
    cos_real = result[:count, :width]
    cos_imag = result[:count, width:]
    sin_real = result[count:, :width]
    sin_imag = result[count:, width:]
    return ((cos_real - sin_imag) * scale, (cos_imag + sin_real) * scale)


def complex_mul(left, right):
    return (left[0] * right[0] - left[1] * right[1], left[0] * right[1] + left[1] * right[0])


def restack(real_part, imag_part, shape):
    return jnp.stack([real_part.reshape(shape), imag_part.reshape(shape)], axis=1).astype(
        jnp.bfloat16
    )


def batched(left, right):
    return jnp.einsum("eij,ejk->eik", left, right, preferred_element_type=jnp.float32)


def plain_device(g_lesser, g_greater, g_free, coulomb):
    ne = lax.axis_size("ea") * g_lesser.shape[0]
    length = 2 * ne
    upper, lower, backward = dft_tables(length, ne)
    tables = (upper, lower)
    scale = 1.0 / (length * ne)
    greater_t = jnp.swapaxes(g_greater, 2, 3)
    lesser_rows, greater_rows = (
        lax.all_to_all(g_lesser, "ea", split_axis=2, concat_axis=0, tiled=True),
        lax.all_to_all(greater_t, "ea", split_axis=2, concat_axis=0, tiled=True),
    )
    spec_lesser = forward(tables, lesser_rows, -1.0)
    element_shape = (ne, lesser_rows.shape[2], lesser_rows.shape[3])
    spec_greater = forward(tables, greater_rows, 1.0)
    joined = complex_mul(spec_lesser, spec_greater)
    polar_real, polar_imag = inverse(backward, joined[0], joined[1], scale)
    polar_rows = restack(polar_real, polar_imag, element_shape)
    polar = lax.all_to_all(polar_rows, "ea", split_axis=0, concat_axis=2, tiled=True)
    mixed_real = jnp.einsum(
        "eij,jk->eik", polar[:, 0], coulomb, preferred_element_type=jnp.float32
    ).astype(jnp.bfloat16)
    mixed_imag = jnp.einsum(
        "eij,jk->eik", polar[:, 1], coulomb, preferred_element_type=jnp.float32
    ).astype(jnp.bfloat16)
    square_real = batched(mixed_real, mixed_real) - batched(mixed_imag, mixed_imag)
    square_imag = batched(mixed_real, mixed_imag) + batched(mixed_imag, mixed_real)
    inner_real = (mixed_real.astype(jnp.float32) + square_real).astype(jnp.bfloat16)
    inner_imag = (mixed_imag.astype(jnp.float32) + square_imag).astype(jnp.bfloat16)
    screen_real = coulomb.astype(jnp.float32)[None] + jnp.einsum(
        "ij,ejk->eik", coulomb, inner_real, preferred_element_type=jnp.float32
    )
    screen_imag = jnp.einsum("ij,ejk->eik", coulomb, inner_imag, preferred_element_type=jnp.float32)
    screen = jnp.stack([screen_real, screen_imag], axis=1).astype(jnp.bfloat16)
    screen_rows = lax.all_to_all(screen, "ea", split_axis=2, concat_axis=0, tiled=True)
    spec_screen = forward(tables, screen_rows, -1.0)
    folded = complex_mul(spec_lesser, spec_screen)
    sigma_real, sigma_imag = inverse(backward, folded[0], folded[1], scale)
    sigma_rows = restack(sigma_real, sigma_imag, element_shape)
    sigma = lax.all_to_all(sigma_rows, "ea", split_axis=0, concat_axis=2, tiled=True)
    free_real = g_free[:, 0]
    free_imag = g_free[:, 1]
    right_real = (batched(sigma[:, 0], free_real) - batched(sigma[:, 1], free_imag)).astype(
        jnp.bfloat16
    )
    right_imag = (batched(sigma[:, 0], free_imag) + batched(sigma[:, 1], free_real)).astype(
        jnp.bfloat16
    )
    out_real = (
        free_real.astype(jnp.float32)
        + batched(free_real, right_real)
        - batched(free_imag, right_imag)
    )
    out_imag = (
        free_imag.astype(jnp.float32)
        + batched(free_real, right_imag)
        + batched(free_imag, right_real)
    )
    return jnp.stack([out_real, out_imag], axis=1).astype(jnp.bfloat16)


def exchange(blocks):
    return lax.all_to_all(blocks, "ea", split_axis=0, concat_axis=0, tiled=True)


def per_device(g_lesser, g_greater, g_free, coulomb):
    block, _, size, _ = g_lesser.shape
    count = lax.axis_size("ea") * block
    if block != 16 or size != 16 * lax.axis_size("ea"):
        return plain_device(g_lesser, g_greater, g_free, coulomb)
    swap = swap_matrix(block)
    tables = spectral_tables(count)
    lesser = exchange(pack_rows(swap, g_lesser))
    greater = exchange(pack_columns(swap, g_greater))
    polar, spec = polarization(tables, lesser, greater)
    screen = exchange(screened(swap, coulomb, exchange(polar)))
    sigma = exchange(self_energy(tables, spec, screen))
    return dyson(swap, sigma, g_free)


def solution(mesh):
    return jax.shard_map(
        per_device,
        mesh=mesh,
        in_specs=(
            P(("bias", "ea"), None, None, None),
            P(("bias", "ea"), None, None, None),
            P(("bias", "ea"), None, None, None),
            P(),
        ),
        out_specs=P(("bias", "ea"), None, None, None),
        check_vma=False,
    )
```

```python
import math

import jax
import jax.numpy as jnp
import numpy as np
from jax import lax
from jax.experimental import pallas as pl
from jax.experimental.pallas import tpu as pltpu
from jax.sharding import Mesh
from jax.sharding import PartitionSpec as P


BF = jnp.bfloat16
F32 = jnp.float32
ROWS = (4, 4, 4, 4)
STARTS = (0, 4, 8, 12)
CHUNKS = len(ROWS)
VMEM = pl.BlockSpec(memory_space=pltpu.VMEM)
SMEM = pl.BlockSpec(memory_space=pltpu.SMEM)


def dot(left, right):
    return jnp.dot(left, right, preferred_element_type=F32)


def swap_matrix(block):
    size = block * block
    row = lax.broadcasted_iota(jnp.int32, (size, size), 0)
    col = lax.broadcasted_iota(jnp.int32, (size, size), 1)
    return ((row % block) * block + row // block == col).astype(BF)


def spectral_tables(count, own_order, mixed_order):
    length = 2 * count
    phase = np.outer(np.arange(length), np.arange(count)) % length
    angle = phase * (2.0 * np.pi / length)
    cosine, sine = lax.optimization_barrier(
        tuple(jnp.asarray(f(angle).astype(np.float32)).astype(BF) for f in (np.cos, np.sin))
    )

    def joined(pick, sign):
        c, s = pick(cosine), sign * pick(sine)
        top = jnp.concatenate([c, -s], axis=1)
        return jnp.concatenate([top, jnp.concatenate([s, c], axis=1)], axis=0)

    def own(table):
        width = count // 4
        return jnp.concatenate(
            [lax.dynamic_slice_in_dim(table, z * width, width, 1) for z in own_order], axis=1
        )

    def mixed(table):
        width = count // len(mixed_order)
        return jnp.concatenate([table[:, z * width : (z + 1) * width] for z in mixed_order], axis=1)

    minus_own = joined(own, -1.0)
    minus_all = joined(lambda table: table, -1.0)
    scale = 1.0 / (length * count)
    tables = dict(
        minus_own=minus_own,
        plus_own=joined(own, 1.0),
        minus_mixed=joined(mixed, -1.0),
        back_own=minus_own.T * BF(scale),
        back_all=minus_all.T * BF(scale),
    )
    return lax.optimization_barrier(tables)


def whole_spec(array):
    return pl.BlockSpec(array.shape, lambda *_: (0,) * array.ndim)


def tile_owners(rows, rest, block, tile):
    several = block // rows
    found = []
    for k in range(several):
        owner = tile * several + k
        found.append((owner // rest % 2, owner // (2 * rest), owner % rest))
    return found


def pack_kernel(swap_ref, pick_ref, lesser_ref, greater_ref, out_ref, turned):
    block = lesser_ref.shape[0]
    size = lesser_ref.shape[-1]
    rest = out_ref.shape[0] // 2
    rows = out_ref.shape[4]
    for e in range(block):
        turned[e] = lax.dot_general(
            pick_ref[...], greater_ref[e, 0], (((1,), (1,)), ((), ())), preferred_element_type=F32
        ).astype(BF)
    for tile in range(rows):
        part = slice(block * tile, block * (tile + 1))
        pair = jnp.concatenate(
            [
                lesser_ref[:, 0, part, :].reshape(block * block, size),
                turned[:, part, :].reshape(block * block, size),
            ],
            axis=1,
        )
        value = dot(swap_ref[...], pair).astype(BF)
        for k, (x, low, r) in enumerate(tile_owners(rows, rest, block, tile)):
            piece = value[k * rows * block : (k + 1) * rows * block]
            for which in range(2):
                out_ref[x * rest + r, low, which, 0] = piece[
                    :, which * size : (which + 1) * size
                ].reshape(rows, block, size)


def pack(swap, lesser, greater, chunk):
    block, _, size, _ = lesser.shape
    rows, start = ROWS[chunk], STARTS[chunk] * block
    count = rows * block
    lanes = 128
    row = lax.broadcasted_iota(jnp.int32, (count, lanes), 0)
    col = lax.broadcasted_iota(jnp.int32, (count, lanes), 1)
    pick = (row + start % lanes == col).astype(BF)
    half = size // block // 2
    return pl.pallas_call(
        pack_kernel,
        grid=(2,),
        in_specs=[
            whole_spec(swap),
            whole_spec(pick),
            pl.BlockSpec((block, 1, count, size), lambda r: (0, r, start // count, 0)),
            pl.BlockSpec((block, 1, size, lanes), lambda r: (0, r, 0, start // lanes)),
        ],
        out_specs=pl.BlockSpec(
            (half, 2, 2, 1, rows, block, size), lambda r: (0, 0, 0, r, 0, 0, 0)
        ),
        out_shape=jax.ShapeDtypeStruct((half, 2, 2, 2, rows, block, size), BF),
        scratch_shapes=[pltpu.VMEM((block, count, size), BF)],
        cost_estimate=pl.CostEstimate(
            flops=12 * block * count * size**2,
            bytes_accessed=8 * block * count * size * 2,
            transcendentals=0,
        ),
        name="pack",
    )(swap, pick, lesser, greater)


def product(left, right):
    half = left.shape[0] // 2
    lr, li = left[:half], left[half:]
    rr, ri = right[:half], right[half:]
    return jnp.concatenate([lr * rr - li * ri, lr * ri + li * rr], axis=0).astype(BF)


PAIR = 2


def side_by_side(columns):
    return jnp.concatenate([jnp.concatenate(pieces, axis=0) for pieces in columns], axis=1)


def each_pair(count, body):
    if count == 1:
        body(0)
    else:
        pl.loop(0, count)(body)


def polar_kernel(minus_ref, plus_ref, back_ref, *refs):
    ins, (out_ref, spec_ref) = refs[:4], refs[4:]
    rows, _, size = ins[0].shape[3:]

    def pair(i):
        def stacked(k):
            return side_by_side(
                [
                    [ref[:, k, r, i * PAIR + a].reshape(-1, size) for r in range(2) for ref in ins]
                    for a in range(PAIR)
                ]
            )

        spec_lesser = dot(minus_ref[...], stacked(0))
        spec_ref[i] = spec_lesser.astype(BF)
        spec_greater = dot(plus_ref[...], stacked(1))
        value = dot(back_ref[...], product(spec_lesser, spec_greater)).astype(BF)
        count = value.shape[0] // 2
        for a in range(PAIR):
            for r in range(2):
                piece = value[count * r : count * (r + 1), a * size : (a + 1) * size]
                out_ref[:, r, i * PAIR + a] = piece.reshape(-1, *out_ref.shape[3:])

    each_pair(rows // PAIR, pair)


def polarization(tables, blocks):
    minus, plus, back = tables["minus_own"], tables["plus_own"], tables["back_all"]
    rest, _, _, rows, block, size = blocks[0].shape
    return pl.pallas_call(
        polar_kernel,
        in_specs=[VMEM] * 7,
        out_specs=[VMEM] * 2,
        out_shape=[
            jax.ShapeDtypeStruct((4 * rest, 2, rows, block, size), BF),
            jax.ShapeDtypeStruct((rows // PAIR, minus.shape[0], PAIR * size), BF),
        ],
        cost_estimate=pl.CostEstimate(
            flops=6 * rows * minus.size * size,
            bytes_accessed=12 * blocks[0].size + 2 * rows * minus.shape[0] * size,
            transcendentals=0,
        ),
        name="polarization",
    )(minus, plus, back, *blocks)


def fold_kernel(place_ref, minus_ref, back_ref, spec_ref, screen_ref, *outs):
    rows, _, size = screen_ref.shape[3:]
    half, low = place_ref[0], place_ref[1]

    def pair(i):
        stacked = side_by_side(
            [
                [screen_ref[:, :, r, i * PAIR + a].reshape(-1, size) for r in range(2)]
                for a in range(PAIR)
            ]
        )
        spec_screen = dot(minus_ref[...], stacked)
        value = dot(back_ref[...], product(spec_ref[i].astype(F32), spec_screen)).astype(BF)
        count = value.shape[0] // 8
        shape = outs[1].shape[:1] + outs[1].shape[3:]
        for a in range(PAIR):
            for r in range(2):
                for k, ref in enumerate(outs):
                    start = count * (4 * r + k)
                    piece = value[start : start + count, a * size : (a + 1) * size].reshape(shape)
                    if k == 0:
                        ref[half, :, low, r, i * PAIR + a] = piece
                    else:
                        ref[:, r, i * PAIR + a] = piece

    each_pair(rows // PAIR, pair)


def self_energy(place, tables, spec, screen):
    minus, back = tables["minus_mixed"], tables["back_own"]
    both, _, _, rows, block, size = screen.shape
    rest = both // 2
    return pl.pallas_call(
        fold_kernel,
        in_specs=[SMEM] + [VMEM] * 4,
        out_specs=[VMEM] * 4,
        out_shape=[jax.ShapeDtypeStruct((2, rest, 2, 2, rows, block, size), BF)]
        + [jax.ShapeDtypeStruct((rest, 2, rows, block, size), BF)] * 3,
        cost_estimate=pl.CostEstimate(
            flops=4 * rows * minus.size * size,
            bytes_accessed=4 * screen.size + 2 * spec.size,
            transcendentals=0,
        ),
        name="self_energy",
    )(place, minus, back, spec, screen)


def to_matrices(swap_ref, whole, tile, pieces):
    block, size = whole.shape[-2:]
    value = dot(swap_ref[...], jnp.concatenate(pieces, axis=1)).astype(BF)
    for r in range(2):
        whole[:, r, tile] = value[:, r * size : (r + 1) * size].reshape(block, block, size)


def from_matrices(swap_ref, whole, tile):
    block, size = whole.shape[-2:]
    pair = [whole[:, r, tile].reshape(block * block, size) for r in range(2)]
    value = dot(swap_ref[...], jnp.concatenate(pair, axis=1)).astype(BF)
    return value[:, :size], value[:, size:]


def each_tile(rows, rest, block, body):
    if rows * rest == block:
        pl.loop(0, rows, unroll=2)(
            lambda tile: body(tile, [(tile % 2, tile // 2, r) for r in range(rest)])
        )
    else:
        for tile in range(rows):
            body(tile, tile_owners(rows, rest, block, tile))


def gather_matrices(swap_ref, refs, whole, rest, order):
    block, size = whole.shape[-2:]

    for ref, start in zip(refs, STARTS):

        def body(tile, owners, ref=ref, start=start):
            pieces = [
                jnp.concatenate([ref[(*order(o), r)].reshape(-1, size) for o in owners], axis=0)
                for r in range(2)
            ]
            to_matrices(swap_ref, whole, start + tile, pieces)

        each_tile(ref.shape[-3], rest, block, body)


def screen_kernel(place_ref, swap_ref, coulomb_ref, *refs):
    ins, owns, aways = refs[:CHUNKS], refs[CHUNKS : 2 * CHUNKS], refs[2 * CHUNKS : 3 * CHUNKS]
    whole = refs[-1]
    size = coulomb_ref.shape[0]
    block = whole.shape[-2]
    rest = ins[0].shape[0] // 4
    low = place_ref[1]
    gather_matrices(swap_ref, ins, whole, rest, lambda o: ((o[0] * 2 + o[1]) * rest + o[2],))
    volts = coulomb_ref[...]

    @pl.loop(0, block, unroll=2)
    def _(w):
        mixed = dot(whole[w].reshape(2 * size, size), volts).astype(BF)
        both = dot(mixed, jnp.concatenate([mixed[:size], mixed[size:]], axis=1))
        by_real, by_imag = both[:, :size], both[:, size:]
        nr = (mixed[:size].astype(F32) + (by_real[:size] - by_imag[size:])).astype(BF)
        ni = (mixed[size:].astype(F32) + (by_imag[:size] + by_real[size:])).astype(BF)
        pair = dot(volts, jnp.concatenate([nr, ni], axis=1))
        whole[w, 0] = (volts.astype(F32) + pair[:, :size]).astype(BF).reshape(whole.shape[2:])
        whole[w, 1] = pair[:, size:].astype(BF).reshape(whole.shape[2:])

    for own_ref, away_ref, start in zip(owns, aways, STARTS):
        rows = own_ref.shape[3]
        each = rows // 2

        def tile(t, own_ref=own_ref, away_ref=away_ref, start=start, rows=rows, each=each):
            width = block // rows
            for k in range(2):
                value = from_matrices(swap_ref, whole, start + (low ^ k) * each + t)
                for r in range(2):
                    piece = value[r].reshape(width, rows, block, size)
                    for i in range(width):
                        if k == 0:
                            own_ref[t * width + i, low, r] = piece[i]
                        else:
                            away_ref[t * width + i, r] = piece[i]

        each_pair(each, tile)


def screened(place, swap, coulomb, polar):
    groups, _, _, block, size = polar[0].shape
    both = groups // 2
    return pl.pallas_call(
        screen_kernel,
        in_specs=[SMEM] + [VMEM] * (2 + CHUNKS),
        out_specs=[VMEM] * (2 * CHUNKS),
        out_shape=[jax.ShapeDtypeStruct((both, 2, 2, rows, block, size), BF) for rows in ROWS]
        + [jax.ShapeDtypeStruct((both, 2, rows, block, size), BF) for rows in ROWS],
        scratch_shapes=[pltpu.VMEM((block, 2, groups, block, size), BF)],
        cost_estimate=pl.CostEstimate(
            flops=20 * block * size**3, bytes_accessed=8 * block * size**2, transcendentals=0
        ),
        name="screened",
    )(place, swap, coulomb, *polar)


def dyson_kernel(swap_ref, *refs):
    sigmas, (free_ref, out_ref, whole) = refs[:CHUNKS], refs[CHUNKS:]
    size = free_ref.shape[-1]
    rest = sigmas[0].shape[0] // 2
    step = pl.program_id(0)

    @pl.when(step == 0)
    def _():
        gather_matrices(swap_ref, sigmas, whole, rest, lambda o: (o[0] * rest + o[2], o[1]))

    for k in range(free_ref.shape[0]):
        sigma = whole[step * free_ref.shape[0] + k].reshape(2 * size, size)
        free = free_ref[k].reshape(2 * size, size)
        both = dot(sigma, jnp.concatenate([free[:size], free[size:]], axis=1))
        by_real, by_imag = both[:, :size], both[:, size:]
        rr = (by_real[:size] - by_imag[size:]).astype(BF)
        ri = (by_imag[:size] + by_real[size:]).astype(BF)
        both = dot(free, jnp.concatenate([rr, ri], axis=1))
        by_real, by_imag = both[:, :size], both[:, size:]
        wide = free.astype(F32)
        out_ref[k, 0] = (wide[:size] + by_real[:size] - by_imag[size:]).astype(BF)
        out_ref[k, 1] = (wide[size:] + by_imag[:size] + by_real[size:]).astype(BF)


def dyson(swap, sigma, free):
    block, size = sigma[0].shape[-2:]
    per = 2
    energy_spec = pl.BlockSpec((per, 2, size, size), lambda e: (e, 0, 0, 0))
    return pl.pallas_call(
        dyson_kernel,
        grid=(block // per,),
        in_specs=[whole_spec(swap)] + [whole_spec(s) for s in sigma] + [energy_spec],
        out_specs=energy_spec,
        out_shape=jax.ShapeDtypeStruct(free.shape, BF),
        scratch_shapes=[pltpu.VMEM((block, 2, size // block, block, size), BF)],
        cost_estimate=pl.CostEstimate(
            flops=18 * block * size**3, bytes_accessed=6 * free.size, transcendentals=0
        ),
        name="dyson",
    )(swap, *sigma, free)


def dft_tables(length, count):
    freq = jnp.arange(length, dtype=jnp.int32)
    places = jnp.arange(count, dtype=jnp.int32)
    phase = freq[:, None] * places[None, :] % length
    angle = phase.astype(jnp.float32) * (2.0 * math.pi / length)
    cosine = jnp.cos(angle)
    sine = jnp.sin(angle)
    stacked = jnp.concatenate([cosine, sine], axis=0)
    upper = stacked.astype(jnp.bfloat16)
    lower = (stacked - upper.astype(jnp.float32)).astype(jnp.bfloat16)
    backward = jnp.concatenate([cosine.T, sine.T], axis=0)
    return (upper, lower, backward)


def forward(tables, block, sign):
    upper, lower = tables
    length = upper.shape[0] // 2
    real_part = block[:, 0].reshape(block.shape[0], -1)
    imag_part = block[:, 1].reshape(block.shape[0], -1)
    width = real_part.shape[1]
    joined = jnp.concatenate([real_part, imag_part], axis=1)
    result = jnp.dot(upper, joined, preferred_element_type=jnp.float32)
    result = result + jnp.dot(lower, joined, preferred_element_type=jnp.float32)
    cos_real = result[:length, :width]
    cos_imag = result[:length, width:]
    sin_real = result[length:, :width]
    sin_imag = result[length:, width:]
    return (cos_real - sign * sin_imag, cos_imag + sign * sin_real)


def inverse(backward, real_part, imag_part, scale):
    count = backward.shape[0] // 2
    width = real_part.shape[1]
    joined = jnp.concatenate([real_part, imag_part], axis=1)
    result = jnp.dot(
        backward, joined, precision=lax.Precision.HIGH, preferred_element_type=jnp.float32
    )
    cos_real = result[:count, :width]
    cos_imag = result[:count, width:]
    sin_real = result[count:, :width]
    sin_imag = result[count:, width:]
    return ((cos_real - sin_imag) * scale, (cos_imag + sin_real) * scale)


def complex_mul(left, right):
    return (left[0] * right[0] - left[1] * right[1], left[0] * right[1] + left[1] * right[0])


def restack(real_part, imag_part, shape):
    return jnp.stack([real_part.reshape(shape), imag_part.reshape(shape)], axis=1).astype(
        jnp.bfloat16
    )


def batched(left, right):
    return jnp.einsum("eij,ejk->eik", left, right, preferred_element_type=jnp.float32)


def plain_device(ea, g_lesser, g_greater, g_free, coulomb):
    ne = lax.axis_size(ea) * g_lesser.shape[0]
    length = 2 * ne
    upper, lower, backward = dft_tables(length, ne)
    tables = (upper, lower)
    scale = 1.0 / (length * ne)
    greater_t = jnp.swapaxes(g_greater, 2, 3)
    lesser_rows, greater_rows = (
        lax.all_to_all(g_lesser, ea, split_axis=2, concat_axis=0, tiled=True),
        lax.all_to_all(greater_t, ea, split_axis=2, concat_axis=0, tiled=True),
    )
    spec_lesser = forward(tables, lesser_rows, -1.0)
    element_shape = (ne, lesser_rows.shape[2], lesser_rows.shape[3])
    spec_greater = forward(tables, greater_rows, 1.0)
    joined = complex_mul(spec_lesser, spec_greater)
    polar_real, polar_imag = inverse(backward, joined[0], joined[1], scale)
    polar_rows = restack(polar_real, polar_imag, element_shape)
    polar = lax.all_to_all(polar_rows, ea, split_axis=0, concat_axis=2, tiled=True)
    mixed_real = jnp.einsum(
        "eij,jk->eik", polar[:, 0], coulomb, preferred_element_type=jnp.float32
    ).astype(jnp.bfloat16)
    mixed_imag = jnp.einsum(
        "eij,jk->eik", polar[:, 1], coulomb, preferred_element_type=jnp.float32
    ).astype(jnp.bfloat16)
    square_real = batched(mixed_real, mixed_real) - batched(mixed_imag, mixed_imag)
    square_imag = batched(mixed_real, mixed_imag) + batched(mixed_imag, mixed_real)
    inner_real = (mixed_real.astype(jnp.float32) + square_real).astype(jnp.bfloat16)
    inner_imag = (mixed_imag.astype(jnp.float32) + square_imag).astype(jnp.bfloat16)
    screen_real = coulomb.astype(jnp.float32)[None] + jnp.einsum(
        "ij,ejk->eik", coulomb, inner_real, preferred_element_type=jnp.float32
    )
    screen_imag = jnp.einsum("ij,ejk->eik", coulomb, inner_imag, preferred_element_type=jnp.float32)
    screen = jnp.stack([screen_real, screen_imag], axis=1).astype(jnp.bfloat16)
    screen_rows = lax.all_to_all(screen, ea, split_axis=2, concat_axis=0, tiled=True)
    spec_screen = forward(tables, screen_rows, -1.0)
    folded = complex_mul(spec_lesser, spec_screen)
    sigma_real, sigma_imag = inverse(backward, folded[0], folded[1], scale)
    sigma_rows = restack(sigma_real, sigma_imag, element_shape)
    sigma = lax.all_to_all(sigma_rows, ea, split_axis=0, concat_axis=2, tiled=True)
    free_real = g_free[:, 0]
    free_imag = g_free[:, 1]
    right_real = (batched(sigma[:, 0], free_real) - batched(sigma[:, 1], free_imag)).astype(
        jnp.bfloat16
    )
    right_imag = (batched(sigma[:, 0], free_imag) + batched(sigma[:, 1], free_real)).astype(
        jnp.bfloat16
    )
    out_real = (
        free_real.astype(jnp.float32)
        + batched(free_real, right_real)
        - batched(free_imag, right_imag)
    )
    out_imag = (
        free_imag.astype(jnp.float32)
        + batched(free_real, right_imag)
        + batched(free_imag, right_real)
    )
    return jnp.stack([out_real, out_imag], axis=1).astype(jnp.bfloat16)


def cube_exchange(blocks):
    return lax.all_to_all(blocks, ("bias", "low", "rest"), split_axis=0, concat_axis=0, tiled=True)


def plane_exchange(blocks):
    return lax.all_to_all(blocks, ("bias", "rest"), split_axis=0, concat_axis=0, tiled=True)


def turn(blocks, step):
    return lax.ppermute(blocks, ("half", "low"), [(i, i ^ step) for i in range(4)])


def cube_device(g_lesser, g_greater, g_free, coulomb):
    block = g_lesser.shape[0]
    rest = lax.axis_size("rest")
    half = lax.axis_index("half").astype(jnp.int32)
    low = lax.axis_index("low").astype(jnp.int32)
    place = jnp.stack([half, low])
    spots = [(half ^ (s >> 1), low ^ (s & 1)) for s in range(4)]
    swap = swap_matrix(block)
    tables = spectral_tables(
        4 * rest * block,
        [2 * h + l for h, l in spots],
        [(x * 2 + l) * rest + r for x in range(2) for r in range(rest) for l in range(2)],
    )
    polar, specs = [], []
    for c in range(CHUNKS):
        packed = pack(swap, g_lesser, g_greater, c)
        own = plane_exchange(packed)
        own = own.reshape((2, rest) + own.shape[1:])
        blocks = [
            lax.dynamic_slice(
                own, (h, 0, l, 0, 0, 0, 0, 0), (1, rest, 1) + own.shape[3:]
            ).reshape((rest,) + own.shape[3:])
            for h, l in spots
        ]
        for s in (1, 2, 3):
            blocks[s] = turn(blocks[s], s)
        p, spec = polarization(tables, blocks)
        polar.append(cube_exchange(p))
        specs.append(spec)
    screens = screened(place, swap, coulomb, polar)
    sigma = []
    for c in range(CHUNKS):
        own, away = screens[c], screens[CHUNKS + c]
        came = turn(away, 1)
        own = lax.dynamic_update_slice(own, came[:, None], (0, 1 - low, 0, 0, 0, 0))
        screen = plane_exchange(own)
        own, *away = self_energy(place, tables, specs[c], screen)
        for s in (1, 2, 3):
            h, l = spots[s]
            came = turn(away[s - 1], s)
            came = came.reshape((1, rest, 1) + came.shape[1:])
            own = lax.dynamic_update_slice(own, came, (h, 0, l, 0, 0, 0, 0))
        sigma.append(plane_exchange(own.reshape((2 * rest,) + own.shape[2:])))
    return dyson(swap, sigma, g_free)


def solution(mesh):
    bias, ea = mesh.shape["bias"], mesh.shape["ea"]
    axes = ("bias", "ea")
    cut = bias == 2 and ea % 4 == 0

    def body(g_lesser, g_greater, g_free, coulomb):
        block, _, size, _ = g_lesser.shape
        if cut and block == 16 and size == block * ea:
            return cube_device(g_lesser, g_greater, g_free, coulomb)
        return plain_device(axes[1:], g_lesser, g_greater, g_free, coulomb)

    if cut:
        mesh = Mesh(mesh.devices.reshape(bias, 2, 2, ea // 4), ("bias", "half", "low", "rest"))
        axes = ("bias", "half", "low", "rest")
    spec = P(axes, None, None, None)
    return jax.shard_map(
        body, mesh=mesh, in_specs=(spec, spec, spec, P()), out_specs=spec, check_vma=False
    )
```

```python
import functools
import math

import jax
import jax.numpy as jnp
import numpy as np
from jax import lax
from jax.experimental import pallas as pl
from jax.experimental.pallas import tpu as pltpu
from jax.sharding import Mesh
from jax.sharding import PartitionSpec as P


BF = jnp.bfloat16
F32 = jnp.float32
ROWS = (4, 4, 4, 4)
STARTS = (0, 4, 8, 12)
CHUNKS = len(ROWS)
VMEM = pl.BlockSpec(memory_space=pltpu.VMEM)
SMEM = pl.BlockSpec(memory_space=pltpu.SMEM)


def dot(left, right):
    return jnp.dot(left, right, preferred_element_type=F32)


def swap_matrix(block):
    size = block * block
    row = lax.broadcasted_iota(jnp.int32, (size, size), 0)
    col = lax.broadcasted_iota(jnp.int32, (size, size), 1)
    return ((row % block) * block + row // block == col).astype(BF)


def spectral_tables(count, own_order, mixed_order):
    length = 2 * count
    phase = np.outer(np.arange(length), np.arange(count)) % length
    angle = phase * (2.0 * np.pi / length)
    cosine, sine = lax.optimization_barrier(
        tuple(jnp.asarray(f(angle).astype(np.float32)).astype(BF) for f in (np.cos, np.sin))
    )

    def joined(pick, sign):
        c, s = pick(cosine), sign * pick(sine)
        top = jnp.concatenate([c, -s], axis=1)
        return jnp.concatenate([top, jnp.concatenate([s, c], axis=1)], axis=0)

    def own(table):
        width = count // 4
        return jnp.concatenate(
            [lax.dynamic_slice_in_dim(table, z * width, width, 1) for z in own_order], axis=1
        )

    def mixed(table):
        width = count // len(mixed_order)
        return jnp.concatenate([table[:, z * width : (z + 1) * width] for z in mixed_order], axis=1)

    minus_own = joined(own, -1.0)
    minus_all = joined(lambda table: table, -1.0)
    scale = 1.0 / (length * count)
    tables = dict(
        minus_own=minus_own,
        plus_own=joined(own, 1.0),
        minus_mixed=joined(mixed, -1.0),
        back_own=minus_own.T * BF(scale),
        back_all=minus_all.T * BF(scale),
    )
    return lax.optimization_barrier(tables)


def whole_spec(array):
    return pl.BlockSpec(array.shape, lambda *_: (0,) * array.ndim)


def tile_owners(rows, rest, block, tile):
    several = block // rows
    found = []
    for k in range(several):
        owner = tile * several + k
        found.append((owner // rest % 2, owner // (2 * rest), owner % rest))
    return found


def pack_kernel(swap_ref, pick_ref, lesser_ref, greater_ref, out_ref, turned):
    block = lesser_ref.shape[0]
    size = lesser_ref.shape[-1]
    rest = out_ref.shape[0] // 2
    rows = out_ref.shape[4]
    for e in range(block):
        turned[e] = lax.dot_general(
            pick_ref[...], greater_ref[e, 0], (((1,), (1,)), ((), ())), preferred_element_type=F32
        ).astype(BF)
    for tile in range(rows):
        part = slice(block * tile, block * (tile + 1))
        pair = jnp.concatenate(
            [
                lesser_ref[:, 0, part, :].reshape(block * block, size),
                turned[:, part, :].reshape(block * block, size),
            ],
            axis=1,
        )
        value = dot(swap_ref[...], pair).astype(BF)
        for k, (x, low, r) in enumerate(tile_owners(rows, rest, block, tile)):
            piece = value[k * rows * block : (k + 1) * rows * block]
            for which in range(2):
                out_ref[x * rest + r, low, which, 0] = piece[
                    :, which * size : (which + 1) * size
                ].reshape(rows, block, size)


def pack(swap, lesser, greater, chunk):
    block, _, size, _ = lesser.shape
    rows, start = ROWS[chunk], STARTS[chunk] * block
    count = rows * block
    lanes = 128
    row = lax.broadcasted_iota(jnp.int32, (count, lanes), 0)
    col = lax.broadcasted_iota(jnp.int32, (count, lanes), 1)
    pick = (row + start % lanes == col).astype(BF)
    half = size // block // 2
    return pl.pallas_call(
        pack_kernel,
        grid=(2,),
        in_specs=[
            whole_spec(swap),
            whole_spec(pick),
            pl.BlockSpec((block, 1, count, size), lambda r: (0, r, start // count, 0)),
            pl.BlockSpec((block, 1, size, lanes), lambda r: (0, r, 0, start // lanes)),
        ],
        out_specs=pl.BlockSpec(
            (half, 2, 2, 1, rows, block, size), lambda r: (0, 0, 0, r, 0, 0, 0)
        ),
        out_shape=jax.ShapeDtypeStruct((half, 2, 2, 2, rows, block, size), BF),
        scratch_shapes=[pltpu.VMEM((block, count, size), BF)],
        cost_estimate=pl.CostEstimate(
            flops=12 * block * count * size**2,
            bytes_accessed=8 * block * count * size * 2,
            transcendentals=0,
        ),
        name="pack",
    )(swap, pick, lesser, greater)


def product(left, right):
    half = left.shape[0] // 2
    lr, li = left[:half], left[half:]
    rr, ri = right[:half], right[half:]
    return jnp.concatenate([lr * rr - li * ri, lr * ri + li * rr], axis=0).astype(BF)


PAIR = 2


def side_by_side(columns):
    return jnp.concatenate([jnp.concatenate(pieces, axis=0) for pieces in columns], axis=1)


def each_pair(count, body):
    if count == 1:
        body(0)
    else:
        pl.loop(0, count)(body)


def polar_kernel(minus_ref, plus_ref, back_ref, *refs):
    ins, (out_ref, spec_ref) = refs[:4], refs[4:]
    rows, _, size = ins[0].shape[3:]

    def pair(i):
        def stacked(k):
            return side_by_side(
                [
                    [ref[:, k, r, i * PAIR + a].reshape(-1, size) for r in range(2) for ref in ins]
                    for a in range(PAIR)
                ]
            )

        spec_lesser = dot(minus_ref[...], stacked(0))
        spec_ref[i] = spec_lesser.astype(BF)
        spec_greater = dot(plus_ref[...], stacked(1))
        value = dot(back_ref[...], product(spec_lesser, spec_greater)).astype(BF)
        count = value.shape[0] // 2
        for a in range(PAIR):
            for r in range(2):
                piece = value[count * r : count * (r + 1), a * size : (a + 1) * size]
                out_ref[:, r, i * PAIR + a] = piece.reshape(-1, *out_ref.shape[3:])

    each_pair(rows // PAIR, pair)


def polarization(tables, blocks):
    minus, plus, back = tables["minus_own"], tables["plus_own"], tables["back_all"]
    rest, _, _, rows, block, size = blocks[0].shape
    return pl.pallas_call(
        polar_kernel,
        in_specs=[VMEM] * 7,
        out_specs=[VMEM] * 2,
        out_shape=[
            jax.ShapeDtypeStruct((4 * rest, 2, rows, block, size), BF),
            jax.ShapeDtypeStruct((rows // PAIR, minus.shape[0], PAIR * size), BF),
        ],
        cost_estimate=pl.CostEstimate(
            flops=6 * rows * minus.size * size,
            bytes_accessed=12 * blocks[0].size + 2 * rows * minus.shape[0] * size,
            transcendentals=0,
        ),
        name="polarization",
    )(minus, plus, back, *blocks)


def fold_kernel(place_ref, minus_ref, back_ref, spec_ref, screen_ref, *outs):
    rows, _, size = screen_ref.shape[3:]
    half, low = place_ref[0], place_ref[1]

    def pair(i):
        stacked = side_by_side(
            [
                [screen_ref[:, :, r, i * PAIR + a].reshape(-1, size) for r in range(2)]
                for a in range(PAIR)
            ]
        )
        spec_screen = dot(minus_ref[...], stacked)
        value = dot(back_ref[...], product(spec_ref[i].astype(F32), spec_screen)).astype(BF)
        count = value.shape[0] // 8
        shape = outs[1].shape[:1] + outs[1].shape[3:]
        for a in range(PAIR):
            for r in range(2):
                for k, ref in enumerate(outs):
                    start = count * (4 * r + k)
                    piece = value[start : start + count, a * size : (a + 1) * size].reshape(shape)
                    if k == 0:
                        ref[half, :, low, r, i * PAIR + a] = piece
                    else:
                        ref[:, r, i * PAIR + a] = piece

    each_pair(rows // PAIR, pair)


def self_energy(place, tables, spec, screen):
    minus, back = tables["minus_mixed"], tables["back_own"]
    both, _, _, rows, block, size = screen.shape
    rest = both // 2
    return pl.pallas_call(
        fold_kernel,
        in_specs=[SMEM] + [VMEM] * 4,
        out_specs=[VMEM] * 4,
        out_shape=[jax.ShapeDtypeStruct((2, rest, 2, 2, rows, block, size), BF)]
        + [jax.ShapeDtypeStruct((rest, 2, rows, block, size), BF)] * 3,
        cost_estimate=pl.CostEstimate(
            flops=4 * rows * minus.size * size,
            bytes_accessed=4 * screen.size + 2 * spec.size,
            transcendentals=0,
        ),
        name="self_energy",
    )(place, minus, back, spec, screen)


def to_matrices(swap_ref, whole, tile, pieces):
    block, size = whole.shape[-2:]
    value = dot(swap_ref[...], jnp.concatenate(pieces, axis=1)).astype(BF)
    for r in range(2):
        whole[:, r, tile] = value[:, r * size : (r + 1) * size].reshape(block, block, size)


def from_matrices(swap_ref, whole, tile):
    block, size = whole.shape[-2:]
    pair = [whole[:, r, tile].reshape(block * block, size) for r in range(2)]
    value = dot(swap_ref[...], jnp.concatenate(pair, axis=1)).astype(BF)
    return value[:, :size], value[:, size:]


def each_tile(rows, rest, block, body):
    if rows * rest == block:
        pl.loop(0, rows, unroll=2)(
            lambda tile: body(tile, [(tile % 2, tile // 2, r) for r in range(rest)])
        )
    else:
        for tile in range(rows):
            body(tile, tile_owners(rows, rest, block, tile))


def gather_chunk(swap_ref, ref, whole, rest, order):
    block, size = whole.shape[-2:]

    def body(tile, owners):
        pieces = [
            jnp.concatenate([ref[(*order(o), r)].reshape(-1, size) for o in owners], axis=0)
            for r in range(2)
        ]
        to_matrices(swap_ref, whole, tile, pieces)

    each_tile(ref.shape[-3], rest, block, body)


def polar_order(rest):
    return lambda o: ((o[0] * 2 + o[1]) * rest + o[2],)


def sigma_order(rest):
    return lambda o: (o[0] * rest + o[2], o[1])


def chunk_shape(blocks):
    rows, block, size = blocks.shape[-3:]
    return (block, 2, rows, block, size)


def gather_kernel(order, rest, swap_ref, ref, out_ref):
    gather_chunk(swap_ref, ref, out_ref, rest, order)


def gathered(swap, blocks, order, rest):
    return pl.pallas_call(
        functools.partial(gather_kernel, order, rest),
        in_specs=[VMEM] * 2,
        out_specs=VMEM,
        out_shape=jax.ShapeDtypeStruct(chunk_shape(blocks), BF),
        cost_estimate=pl.CostEstimate(
            flops=2 * blocks.size * swap.shape[0],
            bytes_accessed=4 * blocks.size,
            transcendentals=0,
        ),
        name="gathered",
    )(swap, blocks)


def stacked_rows(refs, e):
    size = refs[0].shape[-1]
    return jnp.concatenate([ref[e, r].reshape(-1, size) for r in range(2) for ref in refs], axis=0)


def screen_kernel(place_ref, swap_ref, coulomb_ref, *refs):
    ins, owns, aways = refs[:CHUNKS], refs[CHUNKS : 2 * CHUNKS], refs[2 * CHUNKS : 3 * CHUNKS]
    last, whole = refs[3 * CHUNKS :]
    size = coulomb_ref.shape[0]
    block = whole.shape[-2]
    rest = ins[-1].shape[0] // 4
    low = place_ref[1]
    gather_chunk(swap_ref, ins[-1], last, rest, polar_order(rest))
    parts = [*ins[:-1], last]
    volts = coulomb_ref[...]

    @pl.loop(0, block, unroll=2)
    def _(w):
        mixed = dot(stacked_rows(parts, w), volts).astype(BF)
        both = dot(mixed, jnp.concatenate([mixed[:size], mixed[size:]], axis=1))
        by_real, by_imag = both[:, :size], both[:, size:]
        nr = (mixed[:size].astype(F32) + (by_real[:size] - by_imag[size:])).astype(BF)
        ni = (mixed[size:].astype(F32) + (by_imag[:size] + by_real[size:])).astype(BF)
        pair = dot(volts, jnp.concatenate([nr, ni], axis=1))
        whole[w, 0] = (volts.astype(F32) + pair[:, :size]).astype(BF).reshape(whole.shape[2:])
        whole[w, 1] = pair[:, size:].astype(BF).reshape(whole.shape[2:])

    for own_ref, away_ref, start in zip(owns, aways, STARTS):
        rows = own_ref.shape[3]
        each = rows // 2

        def tile(t, own_ref=own_ref, away_ref=away_ref, start=start, rows=rows, each=each):
            width = block // rows
            for k in range(2):
                value = from_matrices(swap_ref, whole, start + (low ^ k) * each + t)
                for r in range(2):
                    piece = value[r].reshape(width, rows, block, size)
                    for i in range(width):
                        if k == 0:
                            own_ref[t * width + i, low, r] = piece[i]
                        else:
                            away_ref[t * width + i, r] = piece[i]

        each_pair(each, tile)


def screened(place, swap, coulomb, polar):
    groups, _, _, block, size = polar[-1].shape
    both = groups // 2
    return pl.pallas_call(
        screen_kernel,
        in_specs=[SMEM] + [VMEM] * (2 + CHUNKS),
        out_specs=[VMEM] * (2 * CHUNKS),
        out_shape=[jax.ShapeDtypeStruct((both, 2, 2, rows, block, size), BF) for rows in ROWS]
        + [jax.ShapeDtypeStruct((both, 2, rows, block, size), BF) for rows in ROWS],
        scratch_shapes=[
            pltpu.VMEM(chunk_shape(polar[-1]), BF),
            pltpu.VMEM((block, 2, groups, block, size), BF),
        ],
        cost_estimate=pl.CostEstimate(
            flops=20 * block * size**3, bytes_accessed=8 * block * size**2, transcendentals=0
        ),
        name="screened",
    )(place, swap, coulomb, *polar)


def dyson_kernel(swap_ref, *refs):
    sigmas, (free_ref, out_ref, last) = refs[:CHUNKS], refs[CHUNKS:]
    size = free_ref.shape[-1]
    rest = sigmas[-1].shape[0] // 2
    step = pl.program_id(0)

    @pl.when(step == 0)
    def _():
        gather_chunk(swap_ref, sigmas[-1], last, rest, sigma_order(rest))

    parts = [*sigmas[:-1], last]
    for k in range(free_ref.shape[0]):
        sigma = stacked_rows(parts, step * free_ref.shape[0] + k)
        free = free_ref[k].reshape(2 * size, size)
        both = dot(sigma, jnp.concatenate([free[:size], free[size:]], axis=1))
        by_real, by_imag = both[:, :size], both[:, size:]
        rr = (by_real[:size] - by_imag[size:]).astype(BF)
        ri = (by_imag[:size] + by_real[size:]).astype(BF)
        both = dot(free, jnp.concatenate([rr, ri], axis=1))
        by_real, by_imag = both[:, :size], both[:, size:]
        wide = free.astype(F32)
        out_ref[k, 0] = (wide[:size] + by_real[:size] - by_imag[size:]).astype(BF)
        out_ref[k, 1] = (wide[size:] + by_imag[:size] + by_real[size:]).astype(BF)


def dyson(swap, sigma, free):
    block, size = sigma[-1].shape[-2:]
    per = 2
    energy_spec = pl.BlockSpec((per, 2, size, size), lambda e: (e, 0, 0, 0))
    return pl.pallas_call(
        dyson_kernel,
        grid=(block // per,),
        in_specs=[VMEM] * (1 + len(sigma)) + [energy_spec],
        out_specs=energy_spec,
        out_shape=jax.ShapeDtypeStruct(free.shape, BF),
        scratch_shapes=[pltpu.VMEM(chunk_shape(sigma[-1]), BF)],
        cost_estimate=pl.CostEstimate(
            flops=18 * block * size**3, bytes_accessed=6 * free.size, transcendentals=0
        ),
        name="dyson",
    )(swap, *sigma, free)


def dft_tables(length, count):
    freq = jnp.arange(length, dtype=jnp.int32)
    places = jnp.arange(count, dtype=jnp.int32)
    phase = freq[:, None] * places[None, :] % length
    angle = phase.astype(jnp.float32) * (2.0 * math.pi / length)
    cosine = jnp.cos(angle)
    sine = jnp.sin(angle)
    stacked = jnp.concatenate([cosine, sine], axis=0)
    upper = stacked.astype(jnp.bfloat16)
    lower = (stacked - upper.astype(jnp.float32)).astype(jnp.bfloat16)
    backward = jnp.concatenate([cosine.T, sine.T], axis=0)
    return (upper, lower, backward)


def forward(tables, block, sign):
    upper, lower = tables
    length = upper.shape[0] // 2
    real_part = block[:, 0].reshape(block.shape[0], -1)
    imag_part = block[:, 1].reshape(block.shape[0], -1)
    width = real_part.shape[1]
    joined = jnp.concatenate([real_part, imag_part], axis=1)
    result = jnp.dot(upper, joined, preferred_element_type=jnp.float32)
    result = result + jnp.dot(lower, joined, preferred_element_type=jnp.float32)
    cos_real = result[:length, :width]
    cos_imag = result[:length, width:]
    sin_real = result[length:, :width]
    sin_imag = result[length:, width:]
    return (cos_real - sign * sin_imag, cos_imag + sign * sin_real)


def inverse(backward, real_part, imag_part, scale):
    count = backward.shape[0] // 2
    width = real_part.shape[1]
    joined = jnp.concatenate([real_part, imag_part], axis=1)
    result = jnp.dot(
        backward, joined, precision=lax.Precision.HIGH, preferred_element_type=jnp.float32
    )
    cos_real = result[:count, :width]
    cos_imag = result[:count, width:]
    sin_real = result[count:, :width]
    sin_imag = result[count:, width:]
    return ((cos_real - sin_imag) * scale, (cos_imag + sin_real) * scale)


def complex_mul(left, right):
    return (left[0] * right[0] - left[1] * right[1], left[0] * right[1] + left[1] * right[0])


def restack(real_part, imag_part, shape):
    return jnp.stack([real_part.reshape(shape), imag_part.reshape(shape)], axis=1).astype(
        jnp.bfloat16
    )


def batched(left, right):
    return jnp.einsum("eij,ejk->eik", left, right, preferred_element_type=jnp.float32)


def plain_device(ea, g_lesser, g_greater, g_free, coulomb):
    ne = lax.axis_size(ea) * g_lesser.shape[0]
    length = 2 * ne
    upper, lower, backward = dft_tables(length, ne)
    tables = (upper, lower)
    scale = 1.0 / (length * ne)
    greater_t = jnp.swapaxes(g_greater, 2, 3)
    lesser_rows, greater_rows = (
        lax.all_to_all(g_lesser, ea, split_axis=2, concat_axis=0, tiled=True),
        lax.all_to_all(greater_t, ea, split_axis=2, concat_axis=0, tiled=True),
    )
    spec_lesser = forward(tables, lesser_rows, -1.0)
    element_shape = (ne, lesser_rows.shape[2], lesser_rows.shape[3])
    spec_greater = forward(tables, greater_rows, 1.0)
    joined = complex_mul(spec_lesser, spec_greater)
    polar_real, polar_imag = inverse(backward, joined[0], joined[1], scale)
    polar_rows = restack(polar_real, polar_imag, element_shape)
    polar = lax.all_to_all(polar_rows, ea, split_axis=0, concat_axis=2, tiled=True)
    mixed_real = jnp.einsum(
        "eij,jk->eik", polar[:, 0], coulomb, preferred_element_type=jnp.float32
    ).astype(jnp.bfloat16)
    mixed_imag = jnp.einsum(
        "eij,jk->eik", polar[:, 1], coulomb, preferred_element_type=jnp.float32
    ).astype(jnp.bfloat16)
    square_real = batched(mixed_real, mixed_real) - batched(mixed_imag, mixed_imag)
    square_imag = batched(mixed_real, mixed_imag) + batched(mixed_imag, mixed_real)
    inner_real = (mixed_real.astype(jnp.float32) + square_real).astype(jnp.bfloat16)
    inner_imag = (mixed_imag.astype(jnp.float32) + square_imag).astype(jnp.bfloat16)
    screen_real = coulomb.astype(jnp.float32)[None] + jnp.einsum(
        "ij,ejk->eik", coulomb, inner_real, preferred_element_type=jnp.float32
    )
    screen_imag = jnp.einsum("ij,ejk->eik", coulomb, inner_imag, preferred_element_type=jnp.float32)
    screen = jnp.stack([screen_real, screen_imag], axis=1).astype(jnp.bfloat16)
    screen_rows = lax.all_to_all(screen, ea, split_axis=2, concat_axis=0, tiled=True)
    spec_screen = forward(tables, screen_rows, -1.0)
    folded = complex_mul(spec_lesser, spec_screen)
    sigma_real, sigma_imag = inverse(backward, folded[0], folded[1], scale)
    sigma_rows = restack(sigma_real, sigma_imag, element_shape)
    sigma = lax.all_to_all(sigma_rows, ea, split_axis=0, concat_axis=2, tiled=True)
    free_real = g_free[:, 0]
    free_imag = g_free[:, 1]
    right_real = (batched(sigma[:, 0], free_real) - batched(sigma[:, 1], free_imag)).astype(
        jnp.bfloat16
    )
    right_imag = (batched(sigma[:, 0], free_imag) + batched(sigma[:, 1], free_real)).astype(
        jnp.bfloat16
    )
    out_real = (
        free_real.astype(jnp.float32)
        + batched(free_real, right_real)
        - batched(free_imag, right_imag)
    )
    out_imag = (
        free_imag.astype(jnp.float32)
        + batched(free_real, right_imag)
        + batched(free_imag, right_real)
    )
    return jnp.stack([out_real, out_imag], axis=1).astype(jnp.bfloat16)


def cube_exchange(blocks):
    return lax.all_to_all(blocks, ("bias", "low", "rest"), split_axis=0, concat_axis=0, tiled=True)


def plane_exchange(blocks):
    return lax.all_to_all(blocks, ("bias", "rest"), split_axis=0, concat_axis=0, tiled=True)


def turn(blocks, step):
    return lax.ppermute(blocks, ("half", "low"), [(i, i ^ step) for i in range(4)])


def cube_device(g_lesser, g_greater, g_free, coulomb):
    block = g_lesser.shape[0]
    rest = lax.axis_size("rest")
    half = lax.axis_index("half").astype(jnp.int32)
    low = lax.axis_index("low").astype(jnp.int32)
    place = jnp.stack([half, low])
    spots = [(half ^ (s >> 1), low ^ (s & 1)) for s in range(4)]
    swap = swap_matrix(block)
    tables = spectral_tables(
        4 * rest * block,
        [2 * h + l for h, l in spots],
        [(x * 2 + l) * rest + r for x in range(2) for r in range(rest) for l in range(2)],
    )
    polar, specs = [], []
    for c in range(CHUNKS):
        packed = pack(swap, g_lesser, g_greater, c)
        own = plane_exchange(packed)
        own = own.reshape((2, rest) + own.shape[1:])
        blocks = [
            lax.dynamic_slice(
                own, (h, 0, l, 0, 0, 0, 0, 0), (1, rest, 1) + own.shape[3:]
            ).reshape((rest,) + own.shape[3:])
            for h, l in spots
        ]
        for s in (1, 2, 3):
            blocks[s] = turn(blocks[s], s)
        p, spec = polarization(tables, blocks)
        came = cube_exchange(p)
        if c < CHUNKS - 1:
            came = gathered(swap, came, polar_order(rest), rest)
        polar.append(came)
        specs.append(spec)
    screens = screened(place, swap, coulomb, polar)
    sigma = []
    for c in range(CHUNKS):
        own, away = screens[c], screens[CHUNKS + c]
        came = turn(away, 1)
        own = lax.dynamic_update_slice(own, came[:, None], (0, 1 - low, 0, 0, 0, 0))
        screen = plane_exchange(own)
        own, *away = self_energy(place, tables, specs[c], screen)
        for s in (1, 2, 3):
            h, l = spots[s]
            came = turn(away[s - 1], s)
            came = came.reshape((1, rest, 1) + came.shape[1:])
            own = lax.dynamic_update_slice(own, came, (h, 0, l, 0, 0, 0, 0))
        came = plane_exchange(own.reshape((2 * rest,) + own.shape[2:]))
        if c < CHUNKS - 1:
            came = gathered(swap, came, sigma_order(rest), rest)
        sigma.append(came)
    return dyson(swap, sigma, g_free)


def solution(mesh):
    bias, ea = mesh.shape["bias"], mesh.shape["ea"]
    axes = ("bias", "ea")
    cut = bias == 2 and ea % 4 == 0

    def body(g_lesser, g_greater, g_free, coulomb):
        block, _, size, _ = g_lesser.shape
        if cut and block == 16 and size == block * ea:
            return cube_device(g_lesser, g_greater, g_free, coulomb)
        return plain_device(axes[1:], g_lesser, g_greater, g_free, coulomb)

    if cut:
        mesh = Mesh(mesh.devices.reshape(bias, 2, 2, ea // 4), ("bias", "half", "low", "rest"))
        axes = ("bias", "half", "low", "rest")
    spec = P(axes, None, None, None)
    return jax.shard_map(
        body, mesh=mesh, in_specs=(spec, spec, spec, P()), out_specs=spec, check_vma=False
    )
```

```python
import functools
import math

import jax
import jax.numpy as jnp
import numpy as np
from jax import lax
from jax.experimental import pallas as pl
from jax.experimental.pallas import tpu as pltpu
from jax.sharding import Mesh
from jax.sharding import PartitionSpec as P


BF = jnp.bfloat16
F32 = jnp.float32
ROWS = (4, 4, 4, 4)
STARTS = (0, 4, 8, 12)
CHUNKS = len(ROWS)
VMEM = pl.BlockSpec(memory_space=pltpu.VMEM)
SMEM = pl.BlockSpec(memory_space=pltpu.SMEM)


def dot(left, right):
    return jnp.dot(left, right, preferred_element_type=F32)


def swap_matrix(block):
    size = block * block
    row = lax.broadcasted_iota(jnp.int32, (size, size), 0)
    col = lax.broadcasted_iota(jnp.int32, (size, size), 1)
    return ((row % block) * block + row // block == col).astype(BF)


def spectral_tables(count, own_order, mixed_order):
    length = 2 * count
    phase = np.outer(np.arange(length), np.arange(count)) % length
    angle = phase * (2.0 * np.pi / length)
    cosine, sine = lax.optimization_barrier(
        tuple(jnp.asarray(f(angle).astype(np.float32)).astype(BF) for f in (np.cos, np.sin))
    )

    def joined(pick, sign):
        c, s = pick(cosine), sign * pick(sine)
        top = jnp.concatenate([c, -s], axis=1)
        return jnp.concatenate([top, jnp.concatenate([s, c], axis=1)], axis=0)

    def own(table):
        width = count // 4
        return jnp.concatenate(
            [lax.dynamic_slice_in_dim(table, z * width, width, 1) for z in own_order], axis=1
        )

    def mixed(table):
        width = count // len(mixed_order)
        return jnp.concatenate([table[:, z * width : (z + 1) * width] for z in mixed_order], axis=1)

    minus_own = joined(own, -1.0)
    minus_all = joined(lambda table: table, -1.0)
    scale = 1.0 / (length * count)
    tables = dict(
        minus_own=minus_own,
        plus_own=joined(own, 1.0),
        minus_mixed=joined(mixed, -1.0),
        back_own=minus_own.T * BF(scale),
        back_all=minus_all.T * BF(scale),
    )
    return lax.optimization_barrier(tables)


def whole_spec(array):
    return pl.BlockSpec(array.shape, lambda *_: (0,) * array.ndim)


def tile_owners(rows, rest, block, tile):
    several = block // rows
    found = []
    for k in range(several):
        owner = tile * several + k
        found.append((owner // rest % 2, owner // (2 * rest), owner % rest))
    return found


def pack_kernel(swap_ref, pick_ref, lesser_ref, greater_ref, out_ref, turned):
    block = lesser_ref.shape[0]
    size = lesser_ref.shape[-1]
    rest = out_ref.shape[0] // 2
    rows = out_ref.shape[4]
    for e in range(block):
        turned[e] = lax.dot_general(
            pick_ref[...], greater_ref[e, 0], (((1,), (1,)), ((), ())), preferred_element_type=F32
        ).astype(BF)
    for tile in range(rows):
        part = slice(block * tile, block * (tile + 1))
        pair = jnp.concatenate(
            [
                lesser_ref[:, 0, part, :].reshape(block * block, size),
                turned[:, part, :].reshape(block * block, size),
            ],
            axis=1,
        )
        value = dot(swap_ref[...], pair).astype(BF)
        for k, (x, low, r) in enumerate(tile_owners(rows, rest, block, tile)):
            piece = value[k * rows * block : (k + 1) * rows * block]
            for which in range(2):
                out_ref[x * rest + r, low, which, 0] = piece[
                    :, which * size : (which + 1) * size
                ].reshape(rows, block, size)


def pack(swap, lesser, greater, chunk):
    block, _, size, _ = lesser.shape
    rows, start = ROWS[chunk], STARTS[chunk] * block
    count = rows * block
    lanes = 128
    row = lax.broadcasted_iota(jnp.int32, (count, lanes), 0)
    col = lax.broadcasted_iota(jnp.int32, (count, lanes), 1)
    pick = (row + start % lanes == col).astype(BF)
    half = size // block // 2
    return pl.pallas_call(
        pack_kernel,
        grid=(2,),
        in_specs=[
            whole_spec(swap),
            whole_spec(pick),
            pl.BlockSpec((block, 1, count, size), lambda r: (0, r, start // count, 0)),
            pl.BlockSpec((block, 1, size, lanes), lambda r: (0, r, 0, start // lanes)),
        ],
        out_specs=pl.BlockSpec(
            (half, 2, 2, 1, rows, block, size), lambda r: (0, 0, 0, r, 0, 0, 0)
        ),
        out_shape=jax.ShapeDtypeStruct((half, 2, 2, 2, rows, block, size), BF),
        scratch_shapes=[pltpu.VMEM((block, count, size), BF)],
        cost_estimate=pl.CostEstimate(
            flops=12 * block * count * size**2,
            bytes_accessed=8 * block * count * size * 2,
            transcendentals=0,
        ),
        name="pack",
    )(swap, pick, lesser, greater)


def product(left, right):
    half = left.shape[0] // 2
    lr, li = left[:half], left[half:]
    rr, ri = right[:half], right[half:]
    return jnp.concatenate([lr * rr - li * ri, lr * ri + li * rr], axis=0).astype(BF)


PAIR = 2


def side_by_side(columns):
    return jnp.concatenate([jnp.concatenate(pieces, axis=0) for pieces in columns], axis=1)


def each_pair(count, body):
    if count == 1:
        body(0)
    else:
        pl.loop(0, count)(body)


def polar_kernel(minus_ref, plus_ref, back_ref, *refs):
    ins, (out_ref, spec_ref) = refs[:4], refs[4:]
    rows, _, size = ins[0].shape[3:]

    def pair(i):
        def stacked(k):
            return side_by_side(
                [
                    [ref[:, k, r, i * PAIR + a].reshape(-1, size) for r in range(2) for ref in ins]
                    for a in range(PAIR)
                ]
            )

        spec_lesser = dot(minus_ref[...], stacked(0))
        spec_ref[i] = spec_lesser.astype(BF)
        spec_greater = dot(plus_ref[...], stacked(1))
        value = dot(back_ref[...], product(spec_lesser, spec_greater)).astype(BF)
        count = value.shape[0] // 2
        for a in range(PAIR):
            for r in range(2):
                piece = value[count * r : count * (r + 1), a * size : (a + 1) * size]
                out_ref[:, r, i * PAIR + a] = piece.reshape(-1, *out_ref.shape[3:])

    each_pair(rows // PAIR, pair)


def polarization(tables, blocks):
    minus, plus, back = tables["minus_own"], tables["plus_own"], tables["back_all"]
    rest, _, _, rows, block, size = blocks[0].shape
    return pl.pallas_call(
        polar_kernel,
        in_specs=[VMEM] * 7,
        out_specs=[VMEM] * 2,
        out_shape=[
            jax.ShapeDtypeStruct((4 * rest, 2, rows, block, size), BF),
            jax.ShapeDtypeStruct((rows // PAIR, minus.shape[0], PAIR * size), BF),
        ],
        cost_estimate=pl.CostEstimate(
            flops=6 * rows * minus.size * size,
            bytes_accessed=12 * blocks[0].size + 2 * rows * minus.shape[0] * size,
            transcendentals=0,
        ),
        name="polarization",
    )(minus, plus, back, *blocks)


def fold_kernel(place_ref, minus_ref, back_ref, spec_ref, screen_ref, *outs):
    rows, _, size = screen_ref.shape[3:]
    half, low = place_ref[0], place_ref[1]

    def pair(i):
        stacked = side_by_side(
            [
                [screen_ref[:, :, r, i * PAIR + a].reshape(-1, size) for r in range(2)]
                for a in range(PAIR)
            ]
        )
        spec_screen = dot(minus_ref[...], stacked)
        value = dot(back_ref[...], product(spec_ref[i].astype(F32), spec_screen)).astype(BF)
        count = value.shape[0] // 8
        shape = outs[1].shape[:1] + outs[1].shape[3:]
        for a in range(PAIR):
            for r in range(2):
                for k, ref in enumerate(outs):
                    start = count * (4 * r + k)
                    piece = value[start : start + count, a * size : (a + 1) * size].reshape(shape)
                    if k == 0:
                        ref[half, :, low, r, i * PAIR + a] = piece
                    else:
                        ref[:, r, i * PAIR + a] = piece

    each_pair(rows // PAIR, pair)


def self_energy(place, tables, spec, screen):
    minus, back = tables["minus_mixed"], tables["back_own"]
    both, _, _, rows, block, size = screen.shape
    rest = both // 2
    return pl.pallas_call(
        fold_kernel,
        in_specs=[SMEM] + [VMEM] * 4,
        out_specs=[VMEM] * 4,
        out_shape=[jax.ShapeDtypeStruct((2, rest, 2, 2, rows, block, size), BF)]
        + [jax.ShapeDtypeStruct((rest, 2, rows, block, size), BF)] * 3,
        cost_estimate=pl.CostEstimate(
            flops=4 * rows * minus.size * size,
            bytes_accessed=4 * screen.size + 2 * spec.size,
            transcendentals=0,
        ),
        name="self_energy",
    )(place, minus, back, spec, screen)


def to_matrices(swap_ref, whole, tile, pieces):
    block, size = whole.shape[-2:]
    value = dot(swap_ref[...], jnp.concatenate(pieces, axis=1)).astype(BF)
    for r in range(2):
        whole[:, r, tile] = value[:, r * size : (r + 1) * size].reshape(block, block, size)


def from_matrices(swap_ref, whole, tile):
    block, size = whole.shape[-2:]
    pair = [whole[:, r, tile].reshape(block * block, size) for r in range(2)]
    value = dot(swap_ref[...], jnp.concatenate(pair, axis=1)).astype(BF)
    return value[:, :size], value[:, size:]


def each_tile(rows, rest, block, body):
    if rows * rest == block:
        pl.loop(0, rows, unroll=2)(
            lambda tile: body(tile, [(tile % 2, tile // 2, r) for r in range(rest)])
        )
    else:
        for tile in range(rows):
            body(tile, tile_owners(rows, rest, block, tile))


def gather_chunk(swap_ref, ref, whole, rest, order):
    block, size = whole.shape[-2:]

    def body(tile, owners):
        pieces = [
            jnp.concatenate([ref[(*order(o), r)].reshape(-1, size) for o in owners], axis=0)
            for r in range(2)
        ]
        to_matrices(swap_ref, whole, tile, pieces)

    each_tile(ref.shape[-3], rest, block, body)


def polar_order(rest):
    return lambda o: ((o[0] * 2 + o[1]) * rest + o[2],)


def sigma_order(rest):
    return lambda o: (o[0] * rest + o[2], o[1])


def chunk_shape(blocks):
    rows, block, size = blocks.shape[-3:]
    return (block, 2, rows, block, size)


def gather_kernel(order, rest, swap_ref, ref, out_ref):
    gather_chunk(swap_ref, ref, out_ref, rest, order)


def gathered(swap, blocks, order, rest):
    return pl.pallas_call(
        functools.partial(gather_kernel, order, rest),
        in_specs=[VMEM] * 2,
        out_specs=VMEM,
        out_shape=jax.ShapeDtypeStruct(chunk_shape(blocks), BF),
        cost_estimate=pl.CostEstimate(
            flops=2 * blocks.size * swap.shape[0],
            bytes_accessed=4 * blocks.size,
            transcendentals=0,
        ),
        name="gathered",
    )(swap, blocks)


def stacked_rows(refs, e):
    size = refs[0].shape[-1]
    return jnp.concatenate([ref[e, r].reshape(-1, size) for r in range(2) for ref in refs], axis=0)


FIRST = 1


def scatter_chunks(swap_ref, whole, owns, aways, chunks, low):
    block, size = whole.shape[-2:]
    base = STARTS[chunks[0]]
    for own_ref, away_ref, chunk in zip(owns, aways, chunks):
        rows, start = ROWS[chunk], STARTS[chunk] - base
        each, width = rows // 2, block // rows

        def tile(
            t, own_ref=own_ref, away_ref=away_ref, start=start, rows=rows, each=each, width=width
        ):
            for k in range(2):
                value = from_matrices(swap_ref, whole, start + (low ^ k) * each + t)
                for r in range(2):
                    piece = value[r].reshape(width, rows, block, size)
                    for i in range(width):
                        if k == 0:
                            own_ref[t * width + i, low, r] = piece[i]
                        else:
                            away_ref[t * width + i, r] = piece[i]

        each_pair(each, tile)


def put_rows(whole, w, volts, pair, first):
    size = pair.shape[-1] // 2
    count = whole.shape[2] * whole.shape[3]
    rows = volts[first : first + count]
    value = dot(rows, pair)
    whole[w, 0] = (rows.astype(F32) + value[:, :size]).astype(BF).reshape(whole.shape[2:])
    whole[w, 1] = value[:, size:].astype(BF).reshape(whole.shape[2:])


def screen_kernel(place_ref, swap_ref, coulomb_ref, *refs):
    ins, owns, aways = refs[:CHUNKS], refs[CHUNKS:][:FIRST], refs[CHUNKS + FIRST :][:FIRST]
    inner_ref, last, whole = refs[-3:]
    size = coulomb_ref.shape[0]
    rest = ins[-1].shape[0] // 4
    gather_chunk(swap_ref, ins[-1], last, rest, polar_order(rest))
    parts = [*ins[:-1], last]
    volts = coulomb_ref[...]

    @pl.loop(0, whole.shape[0], unroll=2)
    def _(w):
        mixed = dot(stacked_rows(parts, w), volts).astype(BF)
        both = dot(mixed, jnp.concatenate([mixed[:size], mixed[size:]], axis=1))
        by_real, by_imag = both[:, :size], both[:, size:]
        nr = (mixed[:size].astype(F32) + (by_real[:size] - by_imag[size:])).astype(BF)
        ni = (mixed[size:].astype(F32) + (by_imag[:size] + by_real[size:])).astype(BF)
        pair = jnp.concatenate([nr, ni], axis=1)
        inner_ref[w] = pair
        put_rows(whole, w, volts, pair, 0)

    scatter_chunks(swap_ref, whole, owns, aways, range(FIRST), place_ref[1])


def screen_more_kernel(place_ref, swap_ref, coulomb_ref, inner_ref, *refs):
    count = CHUNKS - FIRST
    owns, aways, whole = refs[:count], refs[count:-1], refs[-1]
    volts = coulomb_ref[...]

    @pl.loop(0, whole.shape[0], unroll=2)
    def _(w):
        put_rows(whole, w, volts, inner_ref[w], STARTS[FIRST] * whole.shape[3])

    scatter_chunks(swap_ref, whole, owns, aways, range(FIRST, CHUNKS), place_ref[1])


def screen_shapes(chunks, block, size):
    both = size // block // 2
    return [jax.ShapeDtypeStruct((both, 2, 2, ROWS[c], block, size), BF) for c in chunks] + [
        jax.ShapeDtypeStruct((both, 2, ROWS[c], block, size), BF) for c in chunks
    ]


def screen_scratch(chunks, block, size):
    return pltpu.VMEM((block, 2, sum(ROWS[c] for c in chunks), block, size), BF)


def screened(place, swap, coulomb, polar):
    block, size = polar[-1].shape[-2:]
    chunks = range(FIRST)
    return pl.pallas_call(
        screen_kernel,
        in_specs=[SMEM] + [VMEM] * (2 + CHUNKS),
        out_specs=[VMEM] * (2 * FIRST + 1),
        out_shape=screen_shapes(chunks, block, size)
        + [jax.ShapeDtypeStruct((block, size, 2 * size), BF)],
        scratch_shapes=[
            pltpu.VMEM(chunk_shape(polar[-1]), BF),
            screen_scratch(chunks, block, size),
        ],
        cost_estimate=pl.CostEstimate(
            flops=16 * block * size**3, bytes_accessed=10 * block * size**2, transcendentals=0
        ),
        name="screened",
    )(place, swap, coulomb, *polar)


def screened_more(place, swap, coulomb, inner):
    block, size, _ = inner.shape
    chunks = range(FIRST, CHUNKS)
    return pl.pallas_call(
        screen_more_kernel,
        in_specs=[SMEM] + [VMEM] * 3,
        out_specs=[VMEM] * (2 * len(chunks)),
        out_shape=screen_shapes(chunks, block, size),
        scratch_shapes=[screen_scratch(chunks, block, size)],
        cost_estimate=pl.CostEstimate(
            flops=4 * block * size**3, bytes_accessed=8 * block * size**2, transcendentals=0
        ),
        name="screened_more",
    )(place, swap, coulomb, inner)


def dyson_kernel(swap_ref, *refs):
    sigmas, (free_ref, out_ref, last) = refs[:CHUNKS], refs[CHUNKS:]
    size = free_ref.shape[-1]
    rest = sigmas[-1].shape[0] // 2
    step = pl.program_id(0)

    @pl.when(step == 0)
    def _():
        gather_chunk(swap_ref, sigmas[-1], last, rest, sigma_order(rest))

    parts = [*sigmas[:-1], last]
    for k in range(free_ref.shape[0]):
        sigma = stacked_rows(parts, step * free_ref.shape[0] + k)
        free = free_ref[k].reshape(2 * size, size)
        both = dot(sigma, jnp.concatenate([free[:size], free[size:]], axis=1))
        by_real, by_imag = both[:, :size], both[:, size:]
        rr = (by_real[:size] - by_imag[size:]).astype(BF)
        ri = (by_imag[:size] + by_real[size:]).astype(BF)
        both = dot(free, jnp.concatenate([rr, ri], axis=1))
        by_real, by_imag = both[:, :size], both[:, size:]
        wide = free.astype(F32)
        out_ref[k, 0] = (wide[:size] + by_real[:size] - by_imag[size:]).astype(BF)
        out_ref[k, 1] = (wide[size:] + by_imag[:size] + by_real[size:]).astype(BF)


def dyson(swap, sigma, free):
    block, size = sigma[-1].shape[-2:]
    per = 8
    energy_spec = pl.BlockSpec((per, 2, size, size), lambda e: (e, 0, 0, 0))
    return pl.pallas_call(
        dyson_kernel,
        grid=(block // per,),
        in_specs=[VMEM] * (1 + len(sigma)) + [energy_spec],
        out_specs=energy_spec,
        out_shape=jax.ShapeDtypeStruct(free.shape, BF),
        scratch_shapes=[pltpu.VMEM(chunk_shape(sigma[-1]), BF)],
        cost_estimate=pl.CostEstimate(
            flops=18 * block * size**3, bytes_accessed=6 * free.size, transcendentals=0
        ),
        name="dyson",
    )(swap, *sigma, free)


def dft_tables(length, count):
    freq = jnp.arange(length, dtype=jnp.int32)
    places = jnp.arange(count, dtype=jnp.int32)
    phase = freq[:, None] * places[None, :] % length
    angle = phase.astype(jnp.float32) * (2.0 * math.pi / length)
    cosine = jnp.cos(angle)
    sine = jnp.sin(angle)
    stacked = jnp.concatenate([cosine, sine], axis=0)
    upper = stacked.astype(jnp.bfloat16)
    lower = (stacked - upper.astype(jnp.float32)).astype(jnp.bfloat16)
    backward = jnp.concatenate([cosine.T, sine.T], axis=0)
    return (upper, lower, backward)


def forward(tables, block, sign):
    upper, lower = tables
    length = upper.shape[0] // 2
    real_part = block[:, 0].reshape(block.shape[0], -1)
    imag_part = block[:, 1].reshape(block.shape[0], -1)
    width = real_part.shape[1]
    joined = jnp.concatenate([real_part, imag_part], axis=1)
    result = jnp.dot(upper, joined, preferred_element_type=jnp.float32)
    result = result + jnp.dot(lower, joined, preferred_element_type=jnp.float32)
    cos_real = result[:length, :width]
    cos_imag = result[:length, width:]
    sin_real = result[length:, :width]
    sin_imag = result[length:, width:]
    return (cos_real - sign * sin_imag, cos_imag + sign * sin_real)


def inverse(backward, real_part, imag_part, scale):
    count = backward.shape[0] // 2
    width = real_part.shape[1]
    joined = jnp.concatenate([real_part, imag_part], axis=1)
    result = jnp.dot(
        backward, joined, precision=lax.Precision.HIGH, preferred_element_type=jnp.float32
    )
    cos_real = result[:count, :width]
    cos_imag = result[:count, width:]
    sin_real = result[count:, :width]
    sin_imag = result[count:, width:]
    return ((cos_real - sin_imag) * scale, (cos_imag + sin_real) * scale)


def complex_mul(left, right):
    return (left[0] * right[0] - left[1] * right[1], left[0] * right[1] + left[1] * right[0])


def restack(real_part, imag_part, shape):
    return jnp.stack([real_part.reshape(shape), imag_part.reshape(shape)], axis=1).astype(
        jnp.bfloat16
    )


def batched(left, right):
    return jnp.einsum("eij,ejk->eik", left, right, preferred_element_type=jnp.float32)


def plain_device(ea, g_lesser, g_greater, g_free, coulomb):
    ne = lax.axis_size(ea) * g_lesser.shape[0]
    length = 2 * ne
    upper, lower, backward = dft_tables(length, ne)
    tables = (upper, lower)
    scale = 1.0 / (length * ne)
    greater_t = jnp.swapaxes(g_greater, 2, 3)
    lesser_rows, greater_rows = (
        lax.all_to_all(g_lesser, ea, split_axis=2, concat_axis=0, tiled=True),
        lax.all_to_all(greater_t, ea, split_axis=2, concat_axis=0, tiled=True),
    )
    spec_lesser = forward(tables, lesser_rows, -1.0)
    element_shape = (ne, lesser_rows.shape[2], lesser_rows.shape[3])
    spec_greater = forward(tables, greater_rows, 1.0)
    joined = complex_mul(spec_lesser, spec_greater)
    polar_real, polar_imag = inverse(backward, joined[0], joined[1], scale)
    polar_rows = restack(polar_real, polar_imag, element_shape)
    polar = lax.all_to_all(polar_rows, ea, split_axis=0, concat_axis=2, tiled=True)
    mixed_real = jnp.einsum(
        "eij,jk->eik", polar[:, 0], coulomb, preferred_element_type=jnp.float32
    ).astype(jnp.bfloat16)
    mixed_imag = jnp.einsum(
        "eij,jk->eik", polar[:, 1], coulomb, preferred_element_type=jnp.float32
    ).astype(jnp.bfloat16)
    square_real = batched(mixed_real, mixed_real) - batched(mixed_imag, mixed_imag)
    square_imag = batched(mixed_real, mixed_imag) + batched(mixed_imag, mixed_real)
    inner_real = (mixed_real.astype(jnp.float32) + square_real).astype(jnp.bfloat16)
    inner_imag = (mixed_imag.astype(jnp.float32) + square_imag).astype(jnp.bfloat16)
    screen_real = coulomb.astype(jnp.float32)[None] + jnp.einsum(
        "ij,ejk->eik", coulomb, inner_real, preferred_element_type=jnp.float32
    )
    screen_imag = jnp.einsum("ij,ejk->eik", coulomb, inner_imag, preferred_element_type=jnp.float32)
    screen = jnp.stack([screen_real, screen_imag], axis=1).astype(jnp.bfloat16)
    screen_rows = lax.all_to_all(screen, ea, split_axis=2, concat_axis=0, tiled=True)
    spec_screen = forward(tables, screen_rows, -1.0)
    folded = complex_mul(spec_lesser, spec_screen)
    sigma_real, sigma_imag = inverse(backward, folded[0], folded[1], scale)
    sigma_rows = restack(sigma_real, sigma_imag, element_shape)
    sigma = lax.all_to_all(sigma_rows, ea, split_axis=0, concat_axis=2, tiled=True)
    free_real = g_free[:, 0]
    free_imag = g_free[:, 1]
    right_real = (batched(sigma[:, 0], free_real) - batched(sigma[:, 1], free_imag)).astype(
        jnp.bfloat16
    )
    right_imag = (batched(sigma[:, 0], free_imag) + batched(sigma[:, 1], free_real)).astype(
        jnp.bfloat16
    )
    out_real = (
        free_real.astype(jnp.float32)
        + batched(free_real, right_real)
        - batched(free_imag, right_imag)
    )
    out_imag = (
        free_imag.astype(jnp.float32)
        + batched(free_real, right_imag)
        + batched(free_imag, right_real)
    )
    return jnp.stack([out_real, out_imag], axis=1).astype(jnp.bfloat16)


def cube_exchange(blocks):
    return lax.all_to_all(blocks, ("bias", "low", "rest"), split_axis=0, concat_axis=0, tiled=True)


def plane_exchange(blocks):
    return lax.all_to_all(blocks, ("bias", "rest"), split_axis=0, concat_axis=0, tiled=True)


def turn(blocks, step):
    return lax.ppermute(blocks, ("half", "low"), [(i, i ^ step) for i in range(4)])


def cube_device(g_lesser, g_greater, g_free, coulomb):
    block = g_lesser.shape[0]
    rest = lax.axis_size("rest")
    half = lax.axis_index("half").astype(jnp.int32)
    low = lax.axis_index("low").astype(jnp.int32)
    place = jnp.stack([half, low])
    spots = [(half ^ (s >> 1), low ^ (s & 1)) for s in range(4)]
    swap = swap_matrix(block)
    tables = spectral_tables(
        4 * rest * block,
        [2 * h + l for h, l in spots],
        [(x * 2 + l) * rest + r for x in range(2) for r in range(rest) for l in range(2)],
    )
    polar, specs = [], []
    for c in range(CHUNKS):
        packed = pack(swap, g_lesser, g_greater, c)
        own = plane_exchange(packed)
        own = own.reshape((2, rest) + own.shape[1:])
        blocks = [
            lax.dynamic_slice(
                own, (h, 0, l, 0, 0, 0, 0, 0), (1, rest, 1) + own.shape[3:]
            ).reshape((rest,) + own.shape[3:])
            for h, l in spots
        ]
        for s in (1, 2, 3):
            blocks[s] = turn(blocks[s], s)
        p, spec = polarization(tables, blocks)
        came = cube_exchange(p)
        if c < CHUNKS - 1:
            came = gathered(swap, came, polar_order(rest), rest)
        polar.append(came)
        specs.append(spec)
    *early, inner = screened(place, swap, coulomb, polar)
    late = list(screened_more(place, swap, coulomb, inner))
    owns = early[:FIRST] + late[: CHUNKS - FIRST]
    aways = early[FIRST:] + late[CHUNKS - FIRST :]
    sigma = []
    for c in range(CHUNKS):
        own, away = owns[c], aways[c]
        came = turn(away, 1)
        own = lax.dynamic_update_slice(own, came[:, None], (0, 1 - low, 0, 0, 0, 0))
        screen = plane_exchange(own)
        own, *away = self_energy(place, tables, specs[c], screen)
        for s in (1, 2, 3):
            h, l = spots[s]
            came = turn(away[s - 1], s)
            came = came.reshape((1, rest, 1) + came.shape[1:])
            own = lax.dynamic_update_slice(own, came, (h, 0, l, 0, 0, 0, 0))
        came = plane_exchange(own.reshape((2 * rest,) + own.shape[2:]))
        if c < CHUNKS - 1:
            came = gathered(swap, came, sigma_order(rest), rest)
        sigma.append(came)
    return dyson(swap, sigma, g_free)


def solution(mesh):
    bias, ea = mesh.shape["bias"], mesh.shape["ea"]
    axes = ("bias", "ea")
    cut = bias == 2 and ea % 4 == 0

    def body(g_lesser, g_greater, g_free, coulomb):
        block, _, size, _ = g_lesser.shape
        if cut and block == 16 and size == block * ea:
            return cube_device(g_lesser, g_greater, g_free, coulomb)
        return plain_device(axes[1:], g_lesser, g_greater, g_free, coulomb)

    if cut:
        mesh = Mesh(mesh.devices.reshape(bias, 2, 2, ea // 4), ("bias", "half", "low", "rest"))
        axes = ("bias", "half", "low", "rest")
    spec = P(axes, None, None, None)
    return jax.shard_map(
        body, mesh=mesh, in_specs=(spec, spec, spec, P()), out_specs=spec, check_vma=False
    )
```
